512 devices in a mesh: wide: 64 (over z, x_lo, core), narrow: 8 (over y, x_hi).
Axes of the slice: x: 4 (x_hi: 2, x_lo: 2; x = x_hi * 2 + x_lo), y: 4, z: 16, core: 2. Of those that a mesh axis runs over, the one named last changes fastest.
Arguments:
- features: bfloat16 [512, 64, 8, 192], P('wide', 'narrow'), may hold values from -6 to 6
- weight: bfloat16 [5184, 192], replicated, may hold values from -0.078125 to 0.078125
- voxel_mask: int32 [512, 64, 8], P('wide', 'narrow'), may hold values 0 or 1
- cotangent: bfloat16 [512, 64, 8, 192], P('wide', 'narrow'), may hold values from -16 to 16
Outputs:
- activation: bfloat16 [512, 64, 8, 192], P('wide', 'narrow')
- grad_input: bfloat16 [512, 64, 8, 192], P('wide', 'narrow')
- grad_weight: float32 [192, 5184], P('wide')
The draws below stay inside these ranges and needn't reach their ends.
All inputs are finite; a program needn't handle non-finite values. No bound on the sum of `voxel_mask` on one device may be relied on, other than what follows from the above.
Results may differ from the reference program's by a relative error of at most 0.0049.
Values may be sent and summed in bfloat16 or wider, within the bound.
A program may use at most 64 MiB of HBM per device.

```python
import jax
import jax.numpy as jnp

C = 192
BZ = 8
NX = 512
NY = 64
VOXELS = 262144


def plant(entries, own_key, low, largest):
    place = [jax.random.randint(jax.random.fold_in(own_key, axis), (), 0, length) for axis, length in enumerate(entries.shape)]
    main_axis = entries.shape.index(max(entries.shape))
    neighbour = place[:main_axis] + [(place[main_axis] + 1) % entries.shape[main_axis]] + place[main_axis + 1:]
    return entries.at[tuple(place)].set(low).at[tuple(neighbour)].set(largest)


def spiked(drawn, stream_key, source, target, blocks, factor):
    def block_of(axis_at):
        return (jnp.arange(drawn.shape[axis_at]) // (drawn.shape[axis_at] // blocks)).reshape((-1,) + (1,) * (drawn.ndim - 1 - axis_at))

    first = jax.random.permutation(stream_key, blocks)[block_of(target)]
    far = (block_of(target) + blocks // 2) % blocks
    return jnp.where((block_of(source) == first) | (block_of(source) == far), factor * drawn, drawn)


def block_levels(own_key, dims, pieces, least, high):
    loudness, own = 1.0, jax.random.fold_in(own_key, 6)
    for axis_at, shards_of in pieces:
        steps = jnp.exp(jax.random.uniform(jax.random.fold_in(own, axis_at), (shards_of,), jnp.float32, least / len(pieces), high / len(pieces)))
        loudness = loudness * jnp.repeat(steps, dims[axis_at] // shards_of).reshape([-1 if axis == axis_at else 1 for axis in range(len(dims))])
    return loudness


def bell_draw(stream_key, extent, width, reach, cuts=(), held_as=jnp.bfloat16):
    gain = block_levels(stream_key, extent, cuts, -0.22, 0.18) if cuts else 1.0
    result = jax.random.normal(stream_key, extent, jnp.float32) * width * gain
    return jnp.minimum(jnp.maximum(result, -reach), reach).astype(held_as)


def heavy_noise(own_key, shape, width, reach, shards, heavy, kind=jnp.bfloat16):
    array = width * jax.random.normal(own_key, shape, jnp.float32)
    if shards:
        array = array * block_levels(own_key, shape, shards, -0.22, 0.18)
    return jnp.clip(spiked(array, jax.random.fold_in(own_key, 3), *heavy), -reach, reach).astype(kind)


def setup_inputs(seed: int = 0) -> dict:
    arg_keys = jax.random.split(jax.random.key(seed), 5)
    return {
        "features": bell_draw(arg_keys[0], (NX, NY, BZ, C), 1.0, 6.0, ((0, 64), (1, 8))),
        "weight": bell_draw(arg_keys[1], (27 * C, C), (27 * C) ** -0.5, 0.078125),
        "voxel_mask": plant((jax.random.randint(arg_keys[2], (NX, NY, BZ), 0, 2) < 1).astype(jnp.int32), jax.random.fold_in(arg_keys[2], 1), 0, 1),
        "cotangent": heavy_noise(arg_keys[3], (NX, NY, BZ, C), 1.0, 16.0, ((0, 64), (1, 8)), (0, 3, 64, 4.0)),
    }


def shifted(field, off_a, off_b, off_c):
    padded = jnp.pad(field, ((1, 1), (1, 1), (1, 1), (0, 0)))
    size_x, size_y, size_z = (field.shape[0], field.shape[1], field.shape[2])
    return padded[1 + off_a:1 + off_a + size_x, 1 + off_b:1 + off_b + size_y, 1 + off_c:1 + off_c + size_z, :]

def reference(features, weight, voxel_mask, cotangent):
    channels = features.shape[3]
    live = voxel_mask.astype(jnp.float32).reshape(-1, 1)
    masked = features * voxel_mask.astype(features.dtype)[..., None]
    pre = jnp.zeros((masked.shape[0] * masked.shape[1] * masked.shape[2], channels), jnp.float32)
    tap_index = 0
    for off_a in (-1, 0, 1):
        for off_b in (-1, 0, 1):
            for off_c in (-1, 0, 1):
                block = weight[tap_index * channels:(tap_index + 1) * channels]
                source = shifted(masked, off_a, off_b, off_c).reshape(-1, channels)
                pre = pre + jnp.dot(source, block, preferred_element_type=jnp.float32)
                tap_index += 1
    sig = jax.nn.sigmoid(pre)
    activation = (pre * sig * live).astype(features.dtype).reshape(features.shape)
    slope = sig * (1.0 + pre * (1.0 - sig))
    grad_pre = (cotangent.reshape(-1, channels).astype(jnp.float32) * live * slope).astype(features.dtype)
    grad_grid = grad_pre.reshape(features.shape)
    masked_flat = masked.reshape(-1, channels)
    grad_field = jnp.zeros_like(pre)
    blocks = []
    tap_index = 0
    for off_a in (-1, 0, 1):
        for off_b in (-1, 0, 1):
            for off_c in (-1, 0, 1):
                block = weight[tap_index * channels:(tap_index + 1) * channels]
                back = shifted(grad_grid, -off_a, -off_b, -off_c).reshape(-1, channels)
                grad_field = grad_field + jnp.dot(back, block.T, preferred_element_type=jnp.float32)
                source = shifted(masked, off_a, off_b, off_c).reshape(-1, channels)
                blocks.append(jnp.dot(grad_pre.T, source, preferred_element_type=jnp.float32))
                tap_index += 1
    grad_input = (grad_field * live).astype(features.dtype).reshape(features.shape)
    grad_weight = jnp.concatenate(blocks, axis=1) / jnp.sqrt(jnp.float32(VOXELS))
    return (activation, grad_input, grad_weight)
```

```python
import jax
import jax.numpy as jnp
from jax import lax
from jax.experimental import pallas as pl
from jax.experimental.pallas import tpu as pltpu
from jax.sharding import PartitionSpec as P

C = 192
BF = jnp.bfloat16
F32 = jnp.float32
MESH = pl.DeviceIdType.MESH
WIDE, NARROW = 64, 8


def iota(shape, dim):
    return lax.broadcasted_iota(jnp.int32, shape, dim)


def build_shifts(src, even, odd, w, n):
    def body(x, carry):
        v = src[x].astype(F32)
        yy = iota((10, 8, C), 0)
        zz = iota((10, 8, C), 1)
        x_ok = jnp.logical_and(
            jnp.logical_or(x > 0, w > 0), jnp.logical_or(x < 9, w < WIDE - 1)
        )
        lo = jnp.where(n > 0, 0, 1)
        hi = jnp.where(n < NARROW - 1, 9, 8)
        lo = jnp.where(x_ok, lo, 100)
        v = jnp.where((yy >= lo) & (yy <= hi), v, 0.0)
        for c in range(3):
            if c == 0:
                s = jnp.where(zz == 0, 0.0, pltpu.roll(v, 1, 1))
            elif c == 1:
                s = v
            else:
                s = jnp.where(zz == 7, 0.0, pltpu.roll(v, 7, 1))
            s = s.reshape(80, C)
            even[c, x] = s.astype(BF)
            odd[c, x] = s[8:72].astype(BF)
        return carry

    lax.fori_loop(0, 10, body, 0)


def tap_rows(even, odd, a, b, c):
    if b == 1:
        v = odd[c, a : a + 8]
    else:
        v = even[c, a : a + 8, 8 * b : 8 * b + 64, :]
    return v.reshape(512, C)


def kernel(
    feat_hbm, w_hbm, mask_ref, cot_hbm,
    act_ref, gin_ref, gw_ref,
    wv, cot, halo, ghalo, even, odd, cols, pre, live, gp2, gpt,
    own, sb, rb, s1b, a1, b1, a1b, b1b, tb, zb, fin,
    ra, rby, ra2, rb2, rz, ag,
    lsem, hsend, hrecv, gsend, grecv, csend, crecv,
    asend, arecv, bsend, brecv, a2send, a2recv, b2send, b2recv,
    zsend, zrecv, gsnd, grcv,
):
    w = lax.axis_index("wide")
    n = lax.axis_index("narrow")
    core = w % 2
    xl = (w // 2) % 2
    z = w // 4
    y = n // 2
    xh = n % 2
    x = xh * 2 + xl

    def dev(z_, x_, c_, y_):
        return {"wide": (z_ * 2 + x_ % 2) * 2 + c_, "narrow": y_ * 2 + x_ // 2}

    near = []
    for dw, dn in ((1, 0), (-1, 0), (0, 1), (0, -1), (1, 1), (1, -1), (-1, 1), (-1, -1)):
        near.append(
            (dw, dn, {"wide": (w + dw + WIDE) % WIDE, "narrow": (n + dn + NARROW) % NARROW})
        )
    x_dev = [dev(z, (x + d) % 4, core, y) for d in (1, 2, 3)]
    y_dev = [dev(z, x, core, (y + d) % 4) for d in (1, 2, 3)]
    z_dev = [dev((z + d) % 16, x, core, y) for d in range(1, 16)]
    n_dev = [{"wide": w, "narrow": (n + d) % 8} for d in range(1, 8)]

    barrier = pltpu.get_barrier_semaphore()
    partners = [t[2] for t in near] + x_dev + y_dev + z_dev + n_dev
    for p in partners:
        pl.semaphore_signal(barrier, inc=1, device_id=p, device_id_type=MESH)

    c_feat = pltpu.make_async_copy(feat_hbm, halo.at[1:9, 1:9], lsem.at[0])
    c_w = pltpu.make_async_copy(w_hbm, wv, lsem.at[1])
    c_cot = pltpu.make_async_copy(cot_hbm, cot, lsem.at[2])
    c_feat.start()
    c_w.start()
    c_cot.start()

    m = mask_ref[...].astype(F32).reshape(64, 8).astype(BF)
    pick = (iota((512, 64), 0) // 8 == iota((512, 64), 1)).astype(F32).astype(BF)
    mm = jnp.dot(pick, m, preferred_element_type=F32)
    mm = jnp.where(iota((512, 8), 0) % 8 == iota((512, 8), 1), mm, 0.0).astype(BF)
    live[...] = jnp.dot(mm, jnp.ones((8, C), BF), preferred_element_type=F32)

    c_feat.wait()
    for xx in range(8):
        v = halo[1 + xx, 1:9].astype(F32) * live[64 * xx : 64 * xx + 64, :].reshape(8, 8, C)
        halo[1 + xx, 1:9] = v.astype(BF)

    pl.semaphore_wait(barrier, len(partners))

    def exchange(buf, send, recv):
        copies = []
        for k, (dw, dn, d) in enumerate(near):
            sx = {1: slice(8, 9), -1: slice(1, 2), 0: slice(1, 9)}[dw]
            tx = {1: slice(0, 1), -1: slice(9, 10), 0: slice(1, 9)}[dw]
            sy = {1: slice(8, 9), -1: slice(1, 2), 0: slice(1, 9)}[dn]
            ty = {1: slice(0, 1), -1: slice(9, 10), 0: slice(1, 9)}[dn]
            cp = pltpu.make_async_remote_copy(
                src_ref=buf.at[sx, sy],
                dst_ref=buf.at[tx, ty],
                send_sem=send.at[k],
                recv_sem=recv.at[k],
                device_id=d,
                device_id_type=MESH,
            )
            cp.start()
            copies.append(cp)
        return copies

    halo_copies = exchange(halo, hsend, hrecv)
    cols[:, 5120:5248] = jnp.zeros((512, 128), BF)
    for cp in halo_copies:
        cp.wait()

    build_shifts(halo, even, odd, w, n)
    for t in range(27):
        a, b, c = t // 9, (t // 3) % 3, t % 3
        cols[:, C * t : C * t + C] = tap_rows(even, odd, a, b, c)

    c_w.wait()
    pre[...] = jnp.dot(cols[:, 0:5184], wv[...], preferred_element_type=F32)

    c_cot.wait()
    for xx in range(8):
        rows = slice(64 * xx, 64 * xx + 64)
        pv = pre[rows, :]
        lv = live[rows, :]
        sig = jax.nn.sigmoid(pv)
        act_ref[xx] = (pv * sig * lv).reshape(8, 8, C).astype(BF)
        slope = sig * (1.0 + pv * (1.0 - sig))
        ct = cot[xx].astype(F32).reshape(64, C)
        g = ct * lv * slope
        gp2[rows, :] = g.astype(BF)
        ghalo[1 + xx, 1:9] = g.reshape(8, 8, C).astype(BF)

    g_copies = exchange(ghalo, gsend, grecv)

    r = iota((C, C), 0)
    q = (r >= 96).astype(jnp.int32)
    r = r - 96 * q
    rl = (r >= 48).astype(jnp.int32)
    r = r - 48 * rl
    rk = (r >= 16).astype(jnp.int32) + (r >= 32).astype(jnp.int32)
    rz_ = r - 16 * rk
    rc = jnp.where(q == 1, core, 1 - core)
    rj = 3 * ((rz_ * 2 + rl) * 2 + rc) + rk
    perm = (rj == iota((C, C), 1)).astype(F32).astype(BF)
    gpt[...] = lax.dot_general(
        perm, gp2[...], (((1,), (1,)), ((), ())), preferred_element_type=F32
    ).astype(BF)

    tail = jnp.dot(gpt[...], cols[:, 5120:5248], preferred_element_type=F32)
    for l_ in range(2):
        for m_ in range(8):
            k = m_ % 3
            lo = 48 * l_ + 16 * k
            sb[l_, m_ // 2, m_ % 2, 15] = tail[lo : lo + 16].astype(BF)
            own[l_, m_ // 2, m_ % 2, 15] = tail[96 + lo : 112 + lo]

    def owner(i):
        return (y + 2 + 3 * (i // 2)) % 4, (xh + 1 + i) % 2

    partner = dev(z, x, 1 - core, y)

    def core_copy(i):
        yy, hh = owner(i)
        return pltpu.make_async_remote_copy(
            src_ref=sb.at[:, yy, hh],
            dst_ref=rb.at[:, yy, hh],
            send_sem=csend.at[i],
            recv_sem=crecv.at[i],
            device_id=partner,
            device_id_type=MESH,
        )

    def wgrad(i, carry):
        yy, hh = owner(i)
        col = pl.multiple_of((yy * 2 + hh) * 640, 128)
        o = jnp.dot(gpt[...], cols[:, pl.ds(col, 640)], preferred_element_type=F32)
        for l_ in range(2):
            for k in range(3):
                lo = 48 * l_ + 16 * k
                for t in range(5):
                    sb[l_, yy, hh, 5 * k + t] = o[lo : lo + 16, 128 * t : 128 * t + 128].astype(BF)
                    own[l_, yy, hh, 5 * k + t] = o[96 + lo : 112 + lo, 128 * t : 128 * t + 128]
        core_copy(i).start()
        return carry

    lax.fori_loop(0, 8, wgrad, 0)

    def a_copy(i, l_):
        yy, hh = owner(i)
        xt = hh * 2 + l_
        d = (xt - x + 4) % 4
        return d != 0, pltpu.make_async_remote_copy(
            src_ref=s1b.at[l_, yy, hh, pl.ds(0, 8)],
            dst_ref=ra.at[jnp.maximum(d - 1, 0), yy],
            send_sem=asend.at[i, l_],
            recv_sem=arecv.at[jnp.maximum(d - 1, 0), yy],
            device_id=dev(z, xt, core, y),
            device_id_type=MESH,
        )

    def b_copy(i):
        yy, hh = owner(i)
        d = (yy - y + 4) % 4
        return d != 0, pltpu.make_async_remote_copy(
            src_ref=s1b.at[:, yy, hh, pl.ds(8, 8)],
            dst_ref=rby.at[jnp.maximum(d - 1, 0), :, hh],
            send_sem=bsend.at[i],
            recv_sem=brecv.at[jnp.maximum(d - 1, 0), hh],
            device_id=dev(z, x, core, yy),
            device_id_type=MESH,
        )

    def first(i, carry):
        yy, hh = owner(i)
        core_copy(i).wait()
        for l_ in range(2):
            s = own[l_, yy, hh] + rb[l_, yy, hh].astype(F32)
            own[l_, yy, hh] = s
            s1b[l_, yy, hh] = s.astype(BF)
        for l_ in range(2):
            go, cp = a_copy(i, l_)
            pl.when(go)(cp.start)
        go, cp = b_copy(i)
        pl.when(go)(cp.start)
        return carry

    lax.fori_loop(0, 8, first, 0)

    def first_wait(i, carry):
        for l_ in range(2):
            go, cp = a_copy(i, l_)
            pl.when(go)(cp.wait_send)
        go, cp = b_copy(i)
        pl.when(go)(cp.wait_send)
        return carry

    for d in range(3):
        for yy in range(4):
            pltpu.make_async_remote_copy(
                src_ref=s1b.at[0, yy, 0, pl.ds(0, 8)], dst_ref=ra.at[d, yy],
                send_sem=asend.at[0, 0], recv_sem=arecv.at[d, yy],
                device_id=partner, device_id_type=MESH,
            ).wait_recv()
        for hh in range(2):
            pltpu.make_async_remote_copy(
                src_ref=s1b.at[:, 0, hh, pl.ds(8, 8)], dst_ref=rby.at[d, :, hh],
                send_sem=bsend.at[0], recv_sem=brecv.at[d, hh],
                device_id=partner, device_id_type=MESH,
            ).wait_recv()

    for yy in range(4):
        s = own[xl, yy, xh, 0:8]
        for d in range(3):
            s = s + ra[d, yy].astype(F32)
        a1[yy] = s
        a1b[yy] = s.astype(BF)
    for l_ in range(2):
        for hh in range(2):
            s = own[l_, y, hh, 8:16]
            for d in range(3):
                s = s + rby[d, l_, hh].astype(F32)
            b1[hh * 2 + l_] = s
            b1b[hh * 2 + l_] = s.astype(BF)

    second = []
    for d in range(3):
        second.append(
            pltpu.make_async_remote_copy(
                src_ref=a1b.at[(y + d + 1) % 4], dst_ref=ra2.at[d],
                send_sem=a2send.at[d], recv_sem=a2recv.at[d],
                device_id=y_dev[d], device_id_type=MESH,
            )
        )
        second.append(
            pltpu.make_async_remote_copy(
                src_ref=b1b.at[(x + d + 1) % 4], dst_ref=rb2.at[d],
                send_sem=b2send.at[d], recv_sem=b2recv.at[d],
                device_id=x_dev[d], device_id_type=MESH,
            )
        )
    for cp in second:
        cp.start()
    lax.fori_loop(0, 8, first_wait, 0)
    for cp in second:
        cp.wait()
    sa = a1[y]
    sbb = b1[x]
    for d in range(3):
        sa = sa + ra2[d].astype(F32)
        sbb = sbb + rb2[d].astype(F32)
    tb[0:128] = sa.reshape(128, 128).astype(BF)
    tb[128:256] = sbb.reshape(128, 128).astype(BF)

    rr = iota((256, 256), 0)
    turn = (iota((256, 256), 1) == (rr % 16) * 16 + rr // 16).astype(F32).astype(BF)
    zb[...] = (
        jnp.dot(turn, tb[...], preferred_element_type=F32).astype(BF).reshape(16, 16, 128)
    )
    z_copies = []
    for d in range(15):
        cp = pltpu.make_async_remote_copy(
            src_ref=zb.at[(z + d + 1) % 16], dst_ref=rz.at[d],
            send_sem=zsend.at[d], recv_sem=zrecv.at[d],
            device_id=z_dev[d], device_id_type=MESH,
        )
        z_copies.append(cp)
    for d in (7, 6, 8, 5, 9, 4, 10, 3, 11, 2, 12, 1, 13, 0, 14):
        z_copies[d].start()

    for cp in g_copies:
        cp.wait()
    build_shifts(ghalo, even, odd, w, n)
    pre[...] = jnp.zeros((512, C), F32)
    for t in range(27):
        a, b, c = t // 9, (t // 3) % 3, t % 3
        pre[...] += lax.dot_general(
            tap_rows(even, odd, 2 - a, 2 - b, 2 - c),
            wv[C * t : C * t + C, :],
            (((1,), (1,)), ((), ())),
            preferred_element_type=F32,
        )
    for xx in range(8):
        rows = slice(64 * xx, 64 * xx + 64)
        gin_ref[xx] = (pre[rows, :] * live[rows, :]).reshape(8, 8, C).astype(BF)

    total = zb[z].astype(F32)
    for d in range(15):
        z_copies[d].wait()
        total = total + rz[d].astype(F32)
    fin[...] = total * (1.0 / 512.0)

    g_all = []
    for d in range(7):
        cp = pltpu.make_async_remote_copy(
            src_ref=fin, dst_ref=ag.at[n],
            send_sem=gsnd.at[d], recv_sem=grcv.at[d],
            device_id=n_dev[d], device_id_type=MESH,
        )
        cp.start()
        g_all.append(cp)
    ag[n] = fin[...]
    for cp in g_all:
        cp.wait()
    for m_ in range(8):
        for k in range(3):
            for t in range(5):
                lo = (5 * m_ + t) * 128
                gw_ref[k : k + 1, lo : lo + 128] = ag[m_, 5 * k + t : 5 * k + t + 1, :]
    for k in range(3):
        gw_ref[k : k + 1, 5120:5184] = ag[k, 15:16, 0:64]


def local(features, weight, voxel_mask, cotangent):
    dma = pltpu.SemaphoreType.DMA
    vmem = pltpu.VMEM
    scratch = [
        vmem((27 * C, C), BF),
        vmem((8, 8, 8, C), BF),
        vmem((10, 10, 8, C), BF),
        vmem((10, 10, 8, C), BF),
        vmem((3, 10, 80, C), BF),
        vmem((3, 10, 64, C), BF),
        vmem((512, 5248), BF),
        vmem((512, C), F32),
        vmem((512, C), F32),
        vmem((512, C), BF),
        vmem((C, 512), BF),
        vmem((2, 4, 2, 16, 16, 128), F32),
        vmem((2, 4, 2, 16, 16, 128), BF),
        vmem((2, 4, 2, 16, 16, 128), BF),
        vmem((2, 4, 2, 16, 16, 128), BF),
        vmem((4, 8, 16, 128), F32),
        vmem((4, 8, 16, 128), F32),
        vmem((4, 8, 16, 128), BF),
        vmem((4, 8, 16, 128), BF),
        vmem((256, 128), BF),
        vmem((16, 16, 128), BF),
        vmem((16, 128), F32),
        vmem((3, 4, 8, 16, 128), BF),
        vmem((3, 2, 2, 8, 16, 128), BF),
        vmem((3, 8, 16, 128), BF),
        vmem((3, 8, 16, 128), BF),
        vmem((15, 16, 128), BF),
        vmem((8, 16, 128), F32),
        dma((3,)),
        dma((8,)), dma((8,)), dma((8,)), dma((8,)),
        dma((8,)), dma((8,)),
        dma((8, 2)), dma((3, 4)),
        dma((8,)), dma((3, 2)),
        dma((3,)), dma((3,)), dma((3,)), dma((3,)),
        dma((15,)), dma((15,)),
        dma((7,)), dma((7,)),
    ]
    any_ = pl.BlockSpec(memory_space=pl.ANY)
    vm = pl.BlockSpec(memory_space=pltpu.VMEM)
    return pl.pallas_call(
        kernel,
        name="sparse_conv",
        out_shape=(
            jax.ShapeDtypeStruct((8, 8, 8, C), BF),
            jax.ShapeDtypeStruct((8, 8, 8, C), BF),
            jax.ShapeDtypeStruct((3, 27 * C), F32),
        ),
        in_specs=[any_, any_, vm, any_],
        out_specs=(vm, vm, vm),
        scratch_shapes=scratch,
        compiler_params=pltpu.CompilerParams(
            collective_id=0, has_side_effects=True, vmem_limit_bytes=60 * 1024 * 1024
        ),
    )(features, weight, voxel_mask, cotangent)


def solution(mesh):
    return jax.shard_map(
        local,
        mesh=mesh,
        in_specs=(
            P("wide", "narrow", None, None),
            P(),
            P("wide", "narrow", None),
            P("wide", "narrow", None, None),
        ),
        out_specs=(
            P("wide", "narrow", None, None),
            P("wide", "narrow", None, None),
            P("wide", None),
        ),
        check_vma=False,
    )
```

```python
import jax
import jax.numpy as jnp
from jax import lax
from jax.experimental import pallas as pl
from jax.experimental.pallas import tpu as pltpu
from jax.sharding import PartitionSpec as P

C = 192
BF = jnp.bfloat16
F32 = jnp.float32
MESH = pl.DeviceIdType.MESH
WIDE, NARROW = 64, 8
LAG = 3


def iota(shape, dim):
    return lax.broadcasted_iota(jnp.int32, shape, dim)


def build_shifts(src, even, odd, w, n):
    def body(x, carry):
        v = src[x].astype(F32)
        yy = iota((10, 8, C), 0)
        zz = iota((10, 8, C), 1)
        x_ok = jnp.logical_and(
            jnp.logical_or(x > 0, w > 0), jnp.logical_or(x < 9, w < WIDE - 1)
        )
        lo = jnp.where(n > 0, 0, 1)
        hi = jnp.where(n < NARROW - 1, 9, 8)
        lo = jnp.where(x_ok, lo, 100)
        v = jnp.where((yy >= lo) & (yy <= hi), v, 0.0)
        for c in range(3):
            if c == 0:
                s = jnp.where(zz == 0, 0.0, pltpu.roll(v, 1, 1))
            elif c == 1:
                s = v
            else:
                s = jnp.where(zz == 7, 0.0, pltpu.roll(v, 7, 1))
            s = s.reshape(80, C)
            even[c, x] = s.astype(BF)
            odd[c, x] = s[8:72].astype(BF)
        return carry

    lax.fori_loop(0, 10, body, 0)


def tap_rows(even, odd, a, b, c):
    if b == 1:
        v = odd[c, a : a + 8]
    else:
        v = even[c, a : a + 8, 8 * b : 8 * b + 64, :]
    return v.reshape(512, C)


def kernel(
    feat_hbm, w_hbm, mask_hbm, cot_hbm,
    act_ref, gin_ref, ag,
    wv, mask, cot, halo, ghalo, even, odd, cols, pre, live, gp2, gpt,
    own, sb, rb, s1b, a1, b1, a1b, b1b, tb, zb, fin,
    ra, rby, ra2, rb2, rz,
    lsem, hsend, hrecv, gsend, grecv, csend, crecv,
    asend, arecv, bsend, brecv, a2send, a2recv, b2send, b2recv,
    zsend, zrecv, gsnd, grcv, ring,
):
    w = lax.axis_index("wide")
    n = lax.axis_index("narrow")
    core = w % 2
    xl = (w // 2) % 2
    z = w // 4
    y = n // 2
    xh = n % 2
    x = xh * 2 + xl

    def dev(z_, x_, c_, y_):
        return {"wide": (z_ * 2 + x_ % 2) * 2 + c_, "narrow": y_ * 2 + x_ // 2}

    near = []
    for dw, dn in ((1, 0), (-1, 0), (0, 1), (0, -1), (1, 1), (1, -1), (-1, 1), (-1, -1)):
        near.append(
            (dw, dn, {"wide": (w + dw + WIDE) % WIDE, "narrow": (n + dn + NARROW) % NARROW})
        )
    x_dev = [dev(z, (x + d) % 4, core, y) for d in (1, 2, 3)]
    y_dev = [dev(z, x, core, (y + d) % 4) for d in (1, 2, 3)]
    z_dev = [dev((z + d) % 16, x, core, y) for d in range(1, 16)]
    n_dev = [{"wide": w, "narrow": (n + d) % 8} for d in range(1, 8)]

    barrier = pltpu.get_barrier_semaphore()
    partners = [t[2] for t in near] + n_dev + x_dev + [z_dev[0], z_dev[14]]
    for p in partners:
        pl.semaphore_signal(barrier, inc=1, device_id=p, device_id_type=MESH)

    c_feat = pltpu.make_async_copy(feat_hbm, halo.at[1:9, 1:9], lsem.at[0])
    c_w = pltpu.make_async_copy(w_hbm, wv, lsem.at[1])
    c_cot = pltpu.make_async_copy(cot_hbm, cot, lsem.at[2])
    c_mask = pltpu.make_async_copy(mask_hbm, mask, lsem.at[3])
    c_mask.start()
    c_feat.start()
    c_w.start()
    c_cot.start()

    c_mask.wait()
    m = mask[...].astype(F32).reshape(64, 8).astype(BF)
    pick = (iota((512, 64), 0) // 8 == iota((512, 64), 1)).astype(F32).astype(BF)
    mm = jnp.dot(pick, m, preferred_element_type=F32)
    mm = jnp.where(iota((512, 8), 0) % 8 == iota((512, 8), 1), mm, 0.0).astype(BF)
    live[...] = jnp.dot(mm, jnp.ones((8, C), BF), preferred_element_type=F32)

    c_feat.wait()
    for xx in range(8):
        v = halo[1 + xx, 1:9].astype(F32) * live[64 * xx : 64 * xx + 64, :].reshape(8, 8, C)
        halo[1 + xx, 1:9] = v.astype(BF)

    pl.semaphore_wait(barrier, len(partners))

    def tell(d, k):
        for p in (z_dev[d - 1], z_dev[15 - d]):
            pl.semaphore_signal(ring.at[k], inc=1, device_id=p, device_id_type=MESH)

    def met(k):
        pl.semaphore_wait(ring.at[k], 2)

    tell(1, 0)

    def exchange(buf, send, recv):
        copies = []
        for k, (dw, dn, d) in enumerate(near):
            sx = {1: slice(8, 9), -1: slice(1, 2), 0: slice(1, 9)}[dw]
            tx = {1: slice(0, 1), -1: slice(9, 10), 0: slice(1, 9)}[dw]
            sy = {1: slice(8, 9), -1: slice(1, 2), 0: slice(1, 9)}[dn]
            ty = {1: slice(0, 1), -1: slice(9, 10), 0: slice(1, 9)}[dn]
            cp = pltpu.make_async_remote_copy(
                src_ref=buf.at[sx, sy],
                dst_ref=buf.at[tx, ty],
                send_sem=send.at[k],
                recv_sem=recv.at[k],
                device_id=d,
                device_id_type=MESH,
            )
            cp.start()
            copies.append(cp)
        return copies

    halo_copies = exchange(halo, hsend, hrecv)
    cols[:, 5120:5248] = jnp.zeros((512, 128), BF)
    for cp in halo_copies:
        cp.wait()
    met(0)
    tell(2, 1)

    build_shifts(halo, even, odd, w, n)
    for t in range(27):
        a, b, c = t // 9, (t // 3) % 3, t % 3
        cols[:, C * t : C * t + C] = tap_rows(even, odd, a, b, c)

    c_w.wait()
    pre[...] = lax.dot_general(
        cols[:, 0:5184], wv[...], (((1,), (1,)), ((), ())), preferred_element_type=F32
    )

    met(1)
    tell(4, 2)
    c_cot.wait()
    for xx in range(8):
        rows = slice(64 * xx, 64 * xx + 64)
        pv = pre[rows, :]
        lv = live[rows, :]
        sig = jax.nn.sigmoid(pv)
        act_ref[xx] = (pv * sig * lv).reshape(8, 8, C).astype(BF)
        slope = sig * (1.0 + pv * (1.0 - sig))
        ct = cot[xx].astype(F32).reshape(64, C)
        g = ct * lv * slope
        gp2[rows, :] = g.astype(BF)
        ghalo[1 + xx, 1:9] = g.reshape(8, 8, C).astype(BF)

    g_copies = exchange(ghalo, gsend, grecv)

    r = iota((C, C), 0)
    q = (r >= 96).astype(jnp.int32)
    r = r - 96 * q
    rl = (r >= 48).astype(jnp.int32)
    r = r - 48 * rl
    rk = (r >= 16).astype(jnp.int32) + (r >= 32).astype(jnp.int32)
    rz_ = r - 16 * rk
    rc = jnp.where(q == 1, core, 1 - core)
    rj = 3 * ((rz_ * 2 + rl) * 2 + rc) + rk
    perm = (rj == iota((C, C), 1)).astype(F32).astype(BF)
    gpt[...] = lax.dot_general(
        perm, gp2[...], (((1,), (1,)), ((), ())), preferred_element_type=F32
    ).astype(BF)

    tail = jnp.dot(gpt[...], cols[:, 5120:5248], preferred_element_type=F32)
    for l_ in range(2):
        for m_ in range(8):
            k = m_ % 3
            lo = 48 * l_ + 16 * k
            sb[l_, m_ // 2, m_ % 2, 15] = tail[lo : lo + 16].astype(BF)
            own[l_, m_ // 2, m_ % 2, 15] = tail[96 + lo : 112 + lo]

    def owner(i):
        return (y + 2 + 3 * (i // 2)) % 4, (xh + 1 + i) % 2

    partner = dev(z, x, 1 - core, y)

    def core_copy(i):
        yy, hh = owner(i)
        return pltpu.make_async_remote_copy(
            src_ref=sb.at[:, yy, hh],
            dst_ref=rb.at[:, yy, hh],
            send_sem=csend.at[i],
            recv_sem=crecv.at[i],
            device_id=partner,
            device_id_type=MESH,
        )

    def wgrad(i, carry):
        yy, hh = owner(i)
        col = pl.multiple_of((yy * 2 + hh) * 640, 128)
        o = jnp.dot(gpt[...], cols[:, pl.ds(col, 640)], preferred_element_type=F32)
        for l_ in range(2):
            for k in range(3):
                lo = 48 * l_ + 16 * k
                for t in range(5):
                    sb[l_, yy, hh, 5 * k + t] = o[lo : lo + 16, 128 * t : 128 * t + 128].astype(BF)
                    own[l_, yy, hh, 5 * k + t] = o[96 + lo : 112 + lo, 128 * t : 128 * t + 128]
        core_copy(i).start()
        return carry

    def a_copy(i, l_):
        yy, hh = owner(i)
        xt = hh * 2 + l_
        d = (xt - x + 4) % 4
        return d != 0, pltpu.make_async_remote_copy(
            src_ref=s1b.at[l_, yy, hh, pl.ds(0, 8)],
            dst_ref=ra.at[jnp.maximum(d - 1, 0), yy],
            send_sem=asend.at[i, l_],
            recv_sem=arecv.at[jnp.maximum(d - 1, 0), yy],
            device_id=dev(z, xt, core, y),
            device_id_type=MESH,
        )

    def b_copy(i):
        yy, hh = owner(i)
        d = (yy - y + 4) % 4
        return d != 0, pltpu.make_async_remote_copy(
            src_ref=s1b.at[:, yy, hh, pl.ds(8, 8)],
            dst_ref=rby.at[jnp.maximum(d - 1, 0), :, hh],
            send_sem=bsend.at[i],
            recv_sem=brecv.at[jnp.maximum(d - 1, 0), hh],
            device_id=dev(z, x, core, yy),
            device_id_type=MESH,
        )

    def first(i, carry):
        yy, hh = owner(i)
        core_copy(i).wait()
        for l_ in range(2):
            s = own[l_, yy, hh] + rb[l_, yy, hh].astype(F32)
            own[l_, yy, hh] = s
            s1b[l_, yy, hh] = s.astype(BF)
        for l_ in range(2):
            go, cp = a_copy(i, l_)
            pl.when(go)(cp.start)
        go, cp = b_copy(i)
        pl.when(go)(cp.start)
        return carry

    def both(i, carry):
        wgrad(i, carry)
        first(i - LAG, carry)
        return carry

    lax.fori_loop(0, LAG, wgrad, 0)
    lax.fori_loop(LAG, 8, both, 0)
    lax.fori_loop(8 - LAG, 8, first, 0)
    def first_wait(i, carry):
        for l_ in range(2):
            go, cp = a_copy(i, l_)
            pl.when(go)(cp.wait_send)
        go, cp = b_copy(i)
        pl.when(go)(cp.wait_send)
        return carry

    for d in range(3):
        for yy in range(4):
            pltpu.make_async_remote_copy(
                src_ref=s1b.at[0, yy, 0, pl.ds(0, 8)], dst_ref=ra.at[d, yy],
                send_sem=asend.at[0, 0], recv_sem=arecv.at[d, yy],
                device_id=partner, device_id_type=MESH,
            ).wait_recv()
        for hh in range(2):
            pltpu.make_async_remote_copy(
                src_ref=s1b.at[:, 0, hh, pl.ds(8, 8)], dst_ref=rby.at[d, :, hh],
                send_sem=bsend.at[0], recv_sem=brecv.at[d, hh],
                device_id=partner, device_id_type=MESH,
            ).wait_recv()

    for yy in range(4):
        s = own[xl, yy, xh, 0:8]
        for d in range(3):
            s = s + ra[d, yy].astype(F32)
        a1[yy] = s
        a1b[yy] = s.astype(BF)
    for l_ in range(2):
        for hh in range(2):
            s = own[l_, y, hh, 8:16]
            for d in range(3):
                s = s + rby[d, l_, hh].astype(F32)
            b1[hh * 2 + l_] = s
            b1b[hh * 2 + l_] = s.astype(BF)

    second = []
    for d in range(3):
        second.append(
            pltpu.make_async_remote_copy(
                src_ref=a1b.at[(y + d + 1) % 4], dst_ref=ra2.at[d],
                send_sem=a2send.at[d], recv_sem=a2recv.at[d],
                device_id=y_dev[d], device_id_type=MESH,
            )
        )
        second.append(
            pltpu.make_async_remote_copy(
                src_ref=b1b.at[(x + d + 1) % 4], dst_ref=rb2.at[d],
                send_sem=b2send.at[d], recv_sem=b2recv.at[d],
                device_id=x_dev[d], device_id_type=MESH,
            )
        )
    for cp in second:
        cp.start()
    met(2)
    lax.fori_loop(0, 8, first_wait, 0)
    for cp in second:
        cp.wait()
    sa = a1[y]
    sbb = b1[x]
    for d in range(3):
        sa = sa + ra2[d].astype(F32)
        sbb = sbb + rb2[d].astype(F32)
    tb[0:128] = sa.reshape(128, 128).astype(BF)
    tb[128:256] = sbb.reshape(128, 128).astype(BF)

    rr = iota((256, 256), 0)
    turn = (iota((256, 256), 1) == (rr % 16) * 16 + rr // 16).astype(F32).astype(BF)
    zb[...] = (
        jnp.dot(turn, tb[...], preferred_element_type=F32).astype(BF).reshape(16, 16, 128)
    )
    z_copies = []
    for d in range(15):
        cp = pltpu.make_async_remote_copy(
            src_ref=zb.at[(z + d + 1) % 16], dst_ref=rz.at[d],
            send_sem=zsend.at[d], recv_sem=zrecv.at[d],
            device_id=z_dev[d], device_id_type=MESH,
        )
        z_copies.append(cp)
    for d in (7, 6, 8, 5, 9, 4, 10, 3, 11, 2, 12, 1, 13, 0, 14):
        z_copies[d].start()

    for cp in g_copies:
        cp.wait()
    build_shifts(ghalo, even, odd, w, n)
    pre[...] = jnp.zeros((512, C), F32)
    for t in range(27):
        a, b, c = t // 9, (t // 3) % 3, t % 3
        pre[...] += jnp.dot(
            tap_rows(even, odd, 2 - a, 2 - b, 2 - c),
            wv[:, C * t : C * t + C],
            preferred_element_type=F32,
        )
    for xx in range(8):
        rows = slice(64 * xx, 64 * xx + 64)
        gin_ref[xx] = (pre[rows, :] * live[rows, :]).reshape(8, 8, C).astype(BF)

    total = zb[z].astype(F32)
    for d in range(15):
        z_copies[d].wait()
        total = total + rz[d].astype(F32)
    fin[...] = total * (1.0 / 512.0)

    g_all = []
    for d in range(7):
        cp = pltpu.make_async_remote_copy(
            src_ref=fin, dst_ref=ag.at[n],
            send_sem=gsnd.at[d], recv_sem=grcv.at[d],
            device_id=n_dev[d], device_id_type=MESH,
        )
        cp.start()
        g_all.append(cp)
    ag[n] = fin[...]
    for cp in g_all:
        cp.wait()


def finish(act_in, gin_in, ag_in, act_out, gin_out, gw_out, ag, gw, sem):
    copies = [
        pltpu.make_async_copy(ag_in, ag, sem.at[0]),
        pltpu.make_async_copy(act_in, act_out, sem.at[1]),
        pltpu.make_async_copy(gin_in, gin_out, sem.at[2]),
    ]
    for cp in copies:
        cp.start()
    copies[0].wait()
    for m_ in range(8):
        for k in range(3):
            for t in range(5):
                lo = (5 * m_ + t) * 128
                gw[k : k + 1, lo : lo + 128] = ag[m_, 5 * k + t : 5 * k + t + 1, :]
    for k in range(3):
        gw[k : k + 1, 5120:5184] = ag[k, 15:16, 0:64]
    cp = pltpu.make_async_copy(gw, gw_out, sem.at[3])
    cp.start()
    copies[1].wait()
    copies[2].wait()
    cp.wait()


def local(features, weight, voxel_mask, cotangent):
    dma = pltpu.SemaphoreType.DMA
    vmem = pltpu.VMEM
    scratch = [
        vmem((C, 27 * C), BF),
        vmem((8, 8, 8), jnp.int32),
        vmem((8, 8, 8, C), BF),
        vmem((10, 10, 8, C), BF),
        vmem((10, 10, 8, C), BF),
        vmem((3, 10, 80, C), BF),
        vmem((3, 10, 64, C), BF),
        vmem((512, 5248), BF),
        vmem((512, C), F32),
        vmem((512, C), F32),
        vmem((512, C), BF),
        vmem((C, 512), BF),
        vmem((2, 4, 2, 16, 16, 128), F32),
        vmem((2, 4, 2, 16, 16, 128), BF),
        vmem((2, 4, 2, 16, 16, 128), BF),
        vmem((2, 4, 2, 16, 16, 128), BF),
        vmem((4, 8, 16, 128), F32),
        vmem((4, 8, 16, 128), F32),
        vmem((4, 8, 16, 128), BF),
        vmem((4, 8, 16, 128), BF),
        vmem((256, 128), BF),
        vmem((16, 16, 128), BF),
        vmem((16, 128), F32),
        vmem((3, 4, 8, 16, 128), BF),
        vmem((3, 2, 2, 8, 16, 128), BF),
        vmem((3, 8, 16, 128), BF),
        vmem((3, 8, 16, 128), BF),
        vmem((15, 16, 128), BF),
        dma((4,)),
        dma((8,)), dma((8,)), dma((8,)), dma((8,)),
        dma((8,)), dma((8,)),
        dma((8, 2)), dma((3, 4)),
        dma((8,)), dma((3, 2)),
        dma((3,)), dma((3,)), dma((3,)), dma((3,)),
        dma((15,)), dma((15,)),
        dma((7,)), dma((7,)),
        pltpu.SemaphoreType.REGULAR((3,)),
    ]
    any_ = pl.BlockSpec(memory_space=pl.ANY)
    hbm = pl.BlockSpec(memory_space=pltpu.HBM)
    vm = pl.BlockSpec(memory_space=pltpu.VMEM)
    act, gin, blocks = pl.pallas_call(
        kernel,
        name="sparse_conv",
        out_shape=(
            pltpu.VMEM((8, 8, 8, C), BF),
            pltpu.VMEM((8, 8, 8, C), BF),
            pltpu.VMEM((8, 16, 128), F32),
        ),
        in_specs=[hbm] * 4,
        out_specs=(vm, vm, vm),
        scratch_shapes=scratch,
        compiler_params=pltpu.CompilerParams(
            collective_id=0, has_side_effects=True, vmem_limit_bytes=61 * 1024 * 1024
        ),
    )(features, weight.T, voxel_mask, cotangent)
    return pl.pallas_call(
        finish,
        name="finish",
        out_shape=(
            jax.ShapeDtypeStruct((8, 8, 8, C), BF),
            jax.ShapeDtypeStruct((8, 8, 8, C), BF),
            jax.ShapeDtypeStruct((3, 27 * C), F32),
        ),
        in_specs=[any_] * 3,
        out_specs=(any_, any_, any_),
        scratch_shapes=[vmem((8, 16, 128), F32), vmem((3, 27 * C), F32), dma((4,))],
        compiler_params=pltpu.CompilerParams(vmem_limit_bytes=4 * 1024 * 1024),
    )(act, gin, blocks)


def solution(mesh):
    return jax.shard_map(
        local,
        mesh=mesh,
        in_specs=(
            P("wide", "narrow", None, None),
            P(),
            P("wide", "narrow", None),
            P("wide", "narrow", None, None),
        ),
        out_specs=(
            P("wide", "narrow", None, None),
            P("wide", "narrow", None, None),
            P("wide", None),
        ),
        check_vma=False,
    )
```

```python
import jax
import jax.numpy as jnp
from jax import lax
from jax.experimental import pallas as pl
from jax.experimental.pallas import tpu as pltpu
from jax.sharding import PartitionSpec as P

C = 192
BF = jnp.bfloat16
F32 = jnp.float32
MESH = pl.DeviceIdType.MESH
WIDE, NARROW = 64, 8
LAG = 3


def iota(shape, dim):
    return lax.broadcasted_iota(jnp.int32, shape, dim)


def build_shifts(src, even, odd, w, n):
    def body(x, carry):
        v = src[x].astype(F32)
        yy = iota((10, 8, C), 0)
        zz = iota((10, 8, C), 1)
        x_ok = jnp.logical_and(
            jnp.logical_or(x > 0, w > 0), jnp.logical_or(x < 9, w < WIDE - 1)
        )
        lo = jnp.where(n > 0, 0, 1)
        hi = jnp.where(n < NARROW - 1, 9, 8)
        lo = jnp.where(x_ok, lo, 100)
        v = jnp.where((yy >= lo) & (yy <= hi), v, 0.0)
        for c in range(3):
            if c == 0:
                s = jnp.where(zz == 0, 0.0, pltpu.roll(v, 1, 1))
            elif c == 1:
                s = v
            else:
                s = jnp.where(zz == 7, 0.0, pltpu.roll(v, 7, 1))
            s = s.reshape(80, C)
            even[c, x] = s.astype(BF)
            odd[c, x] = s[8:72].astype(BF)
        return carry

    lax.fori_loop(0, 10, body, 0)


def tap_rows(even, odd, a, b, c):
    if b == 1:
        v = odd[c, a : a + 8]
    else:
        v = even[c, a : a + 8, 8 * b : 8 * b + 64, :]
    return v.reshape(512, C)


def kernel(
    feat_hbm, w_hbm, mask_hbm, cot_hbm,
    act_ref, gin_ref, ag,
    wv, mask, cot, halo, ghalo, even, odd, cols, pre, live, gp2, gpt,
    own, sb, rb, s1b, a1, b1, a1b, b1b, tb, zb, fin,
    fl, fr, fd, fu, rpa, rma, rpb, rmb, ra2, rb2, rz, permv, turnv,
    lsem, hsend, hrecv, gsend, grecv, csend, crecv,
    ads, adr, ars, arr, ass, asr, bds, bdr, brs, brr, bss, bsr, a2send, a2recv, b2send, b2recv,
    zsend, zrecv, gsnd, grcv, ring,
):
    w = lax.axis_index("wide")
    n = lax.axis_index("narrow")
    core = w % 2
    xl = (w // 2) % 2
    z = w // 4
    y = n // 2
    xh = n % 2
    x = xh * 2 + xl

    def dev(z_, x_, c_, y_):
        return {"wide": (z_ * 2 + x_ % 2) * 2 + c_, "narrow": y_ * 2 + x_ // 2}

    near = []
    for dw, dn in ((1, 1), (1, -1), (-1, 1), (-1, -1), (0, 1), (0, -1), (1, 0), (-1, 0)):
        near.append(
            (dw, dn, {"wide": (w + dw + WIDE) % WIDE, "narrow": (n + dn + NARROW) % NARROW})
        )
    x_dev = [dev(z, (x + d) % 4, core, y) for d in (1, 2, 3)]
    y_dev = [dev(z, x, core, (y + d) % 4) for d in (1, 2, 3)]
    z_dev = [dev((z + d) % 16, x, core, y) for d in range(1, 16)]
    n_dev = [{"wide": w, "narrow": (n + d) % 8} for d in range(1, 8)]

    barrier = pltpu.get_barrier_semaphore()
    partners = [t[2] for t in near] + n_dev + x_dev + [z_dev[0], z_dev[14]]
    for p in partners:
        pl.semaphore_signal(barrier, inc=1, device_id=p, device_id_type=MESH)

    c_feat = pltpu.make_async_copy(feat_hbm, halo.at[1:9, 1:9], lsem.at[0])
    c_w = pltpu.make_async_copy(w_hbm, wv, lsem.at[1])
    c_cot = pltpu.make_async_copy(cot_hbm, cot, lsem.at[2])
    c_mask = pltpu.make_async_copy(mask_hbm, mask, lsem.at[3])
    c_mask.start()
    c_feat.start()
    c_w.start()
    c_cot.start()

    c_mask.wait()
    m = mask[...].astype(F32).reshape(64, 8).astype(BF)
    pick = (iota((512, 64), 0) // 8 == iota((512, 64), 1)).astype(F32).astype(BF)
    mm = jnp.dot(pick, m, preferred_element_type=F32)
    mm = jnp.where(iota((512, 8), 0) % 8 == iota((512, 8), 1), mm, 0.0).astype(BF)
    live[...] = jnp.dot(mm, jnp.ones((8, C), BF), preferred_element_type=F32)

    c_feat.wait()
    for xx in range(8):
        v = halo[1 + xx, 1:9].astype(F32) * live[64 * xx : 64 * xx + 64, :].reshape(8, 8, C)
        halo[1 + xx, 1:9] = v.astype(BF)

    pl.semaphore_wait(barrier, len(partners))

    def tell(d, k):
        for p in (z_dev[d - 1], z_dev[15 - d]):
            pl.semaphore_signal(ring.at[k], inc=1, device_id=p, device_id_type=MESH)

    def met(k):
        pl.semaphore_wait(ring.at[k], 2)

    tell(1, 0)

    def exchange(buf, send, recv):
        copies = []
        for k, (dw, dn, d) in enumerate(near):
            sx = {1: slice(8, 9), -1: slice(1, 2), 0: slice(1, 9)}[dw]
            tx = {1: slice(0, 1), -1: slice(9, 10), 0: slice(1, 9)}[dw]
            sy = {1: slice(8, 9), -1: slice(1, 2), 0: slice(1, 9)}[dn]
            ty = {1: slice(0, 1), -1: slice(9, 10), 0: slice(1, 9)}[dn]
            cp = pltpu.make_async_remote_copy(
                src_ref=buf.at[sx, sy],
                dst_ref=buf.at[tx, ty],
                send_sem=send.at[k],
                recv_sem=recv.at[k],
                device_id=d,
                device_id_type=MESH,
            )
            cp.start()
            copies.append(cp)
        return copies

    halo_copies = exchange(halo, hsend, hrecv)
    cols[:, 5120:5248] = jnp.zeros((512, 128), BF)
    r = iota((C, C), 0)
    q = (r >= 96).astype(jnp.int32)
    r = r - 96 * q
    rl = (r >= 48).astype(jnp.int32)
    r = r - 48 * rl
    rk = (r >= 16).astype(jnp.int32) + (r >= 32).astype(jnp.int32)
    rz_ = r - 16 * rk
    rc = jnp.where(q == 1, core, 1 - core)
    rj = 3 * ((rz_ * 2 + rl) * 2 + rc) + rk
    permv[...] = (rj == iota((C, C), 1)).astype(F32).astype(BF)
    rr = iota((256, 256), 0)
    turnv[...] = (iota((256, 256), 1) == (rr % 16) * 16 + rr // 16).astype(F32).astype(BF)

    for cp in halo_copies:
        cp.wait()
    met(0)
    tell(2, 1)

    build_shifts(halo, even, odd, w, n)
    for t in range(27):
        a, b, c = t // 9, (t // 3) % 3, t % 3
        cols[:, C * t : C * t + C] = tap_rows(even, odd, a, b, c)

    c_w.wait()
    pre[...] = lax.dot_general(
        cols[:, 0:5184], wv[...], (((1,), (1,)), ((), ())), preferred_element_type=F32
    )

    met(1)
    tell(4, 2)
    c_cot.wait()
    for xx in range(8):
        rows = slice(64 * xx, 64 * xx + 64)
        pv = pre[rows, :]
        lv = live[rows, :]
        sig = jax.nn.sigmoid(pv)
        act_ref[xx] = (pv * sig * lv).reshape(8, 8, C).astype(BF)
        slope = sig * (1.0 + pv * (1.0 - sig))
        ct = cot[xx].astype(F32).reshape(64, C)
        g = ct * lv * slope
        gp2[rows, :] = g.astype(BF)
        ghalo[1 + xx, 1:9] = g.reshape(8, 8, C).astype(BF)

    g_copies = exchange(ghalo, gsend, grecv)

    gpt[...] = lax.dot_general(
        permv[...], gp2[...], (((1,), (1,)), ((), ())), preferred_element_type=F32
    ).astype(BF)

    tail = jnp.dot(gpt[...], cols[:, 5120:5248], preferred_element_type=F32)
    for l_ in range(2):
        for m_ in range(8):
            k = m_ % 3
            lo = 48 * l_ + 16 * k
            sb[l_, m_ // 2, m_ % 2, 15] = tail[lo : lo + 16].astype(BF)
            own[l_, m_ // 2, m_ % 2, 15] = tail[96 + lo : 112 + lo]

    def owner(i):
        return (y + 2 + 3 * (i % 4)) % 4, (xh + 1 + i // 4) % 2

    partner = dev(z, x, 1 - core, y)

    def core_copy(i):
        yy, hh = owner(i)
        return pltpu.make_async_remote_copy(
            src_ref=sb.at[:, yy, hh],
            dst_ref=rb.at[:, yy, hh],
            send_sem=csend.at[i],
            recv_sem=crecv.at[i],
            device_id=partner,
            device_id_type=MESH,
        )

    def wgrad(i, carry):
        yy, hh = owner(i)
        col = pl.multiple_of((yy * 2 + hh) * 640, 128)
        o = jnp.dot(gpt[...], cols[:, pl.ds(col, 640)], preferred_element_type=F32)
        for l_ in range(2):
            for k in range(3):
                lo = 48 * l_ + 16 * k
                for t in range(5):
                    sb[l_, yy, hh, 5 * k + t] = o[lo : lo + 16, 128 * t : 128 * t + 128].astype(BF)
                    own[l_, yy, hh, 5 * k + t] = o[96 + lo : 112 + lo, 128 * t : 128 * t + 128]
        core_copy(i).start()
        return carry

    xp, xo, xm = (x + 1) % 4, (x + 2) % 4, (x + 3) % 4
    yp, yo, ym = (y + 1) % 4, (y + 2) % 4, (y + 3) % 4

    def remote(src, dst, send, recv, d):
        return pltpu.make_async_remote_copy(
            src_ref=src, dst_ref=dst, send_sem=send, recv_sem=recv,
            device_id=d, device_id_type=MESH,
        )

    def a_part(xt, yy, lo):
        return s1b.at[xt % 2, yy, xt // 2, pl.ds(lo, 4)]

    def a_dir(yy):
        return (
            remote(a_part(xp, yy, 4), fl.at[yy, pl.ds(4, 4)], ads.at[0, yy], adr.at[0, yy], x_dev[0]),
            remote(a_part(xm, yy, 0), fr.at[yy, pl.ds(0, 4)], ads.at[1, yy], adr.at[1, yy], x_dev[2]),
        )

    def a_rel(yy):
        return (
            remote(a_part(xo, yy, 0), rpa.at[yy], ars.at[0, yy], arr.at[0, yy], x_dev[0]),
            remote(a_part(xo, yy, 4), rma.at[yy], ars.at[1, yy], arr.at[1, yy], x_dev[2]),
        )

    def b_part(yt, hh, lo):
        return s1b.at[:, yt, hh, pl.ds(lo, 4)]

    def b_dir(hh):
        return (
            remote(b_part(yp, hh, 12), fd.at[:, hh, pl.ds(4, 4)], bds.at[0, hh], bdr.at[0, hh], y_dev[0]),
            remote(b_part(ym, hh, 8), fu.at[:, hh, pl.ds(0, 4)], bds.at[1, hh], bdr.at[1, hh], y_dev[2]),
        )

    def b_rel(hh):
        return (
            remote(b_part(yo, hh, 8), rpb.at[hh], brs.at[0, hh], brr.at[0, hh], y_dev[0]),
            remote(b_part(yo, hh, 12), rmb.at[hh], brs.at[1, hh], brr.at[1, hh], y_dev[2]),
        )

    a_sum = (
        remote(s1b.at[xp % 2, :, xp // 2, pl.ds(0, 4)], fl.at[:, pl.ds(0, 4)], ass.at[0], asr.at[0], x_dev[0]),
        remote(s1b.at[xm % 2, :, xm // 2, pl.ds(4, 4)], fr.at[:, pl.ds(4, 4)], ass.at[1], asr.at[1], x_dev[2]),
    )
    b_sum = (
        remote(s1b.at[:, yp, :, pl.ds(8, 4)], fd.at[:, :, pl.ds(0, 4)], bss.at[0], bsr.at[0], y_dev[0]),
        remote(s1b.at[:, ym, :, pl.ds(12, 4)], fu.at[:, :, pl.ds(4, 4)], bss.at[1], bsr.at[1], y_dev[2]),
    )

    def first(i, carry):
        yy, hh = owner(i)
        core_copy(i).wait()
        for l_ in range(2):
            s = own[l_, yy, hh] + rb[l_, yy, hh].astype(F32)
            own[l_, yy, hh] = s
            s1b[l_, yy, hh] = s.astype(BF)
        for l_ in range(2):
            xt = hh * 2 + l_
            pl.when(xt == xo)(lambda: [cp.start() for cp in a_rel(yy)] and None)
            pl.when(xt == xp)(a_dir(yy)[0].start)
            pl.when(xt == xm)(a_dir(yy)[1].start)
        pl.when(yy == yo)(lambda: [cp.start() for cp in b_rel(hh)] and None)
        pl.when(yy == yp)(b_dir(hh)[0].start)
        pl.when(yy == ym)(b_dir(hh)[1].start)
        return carry

    def both(i, carry):
        wgrad(i, carry)
        first(i - LAG, carry)
        return carry

    lax.fori_loop(0, LAG, wgrad, 0)
    lax.fori_loop(LAG, 8, both, 0)
    lax.fori_loop(8 - LAG, 8, first, 0)
    for yy in range(4):
        for cp in a_rel(yy):
            cp.wait_recv()
        s = own[xp % 2, yy, xp // 2, 0:4] + rpa[yy].astype(F32)
        s1b[xp % 2, yy, xp // 2, 0:4] = s.astype(BF)
        s = own[xm % 2, yy, xm // 2, 4:8] + rma[yy].astype(F32)
        s1b[xm % 2, yy, xm // 2, 4:8] = s.astype(BF)
    for cp in a_sum:
        cp.start()
    for hh in range(2):
        for cp in b_rel(hh):
            cp.wait_recv()
        for l_ in range(2):
            s = own[l_, yp, hh, 8:12] + rpb[hh, l_].astype(F32)
            s1b[l_, yp, hh, 8:12] = s.astype(BF)
            s = own[l_, ym, hh, 12:16] + rmb[hh, l_].astype(F32)
            s1b[l_, ym, hh, 12:16] = s.astype(BF)
    for cp in b_sum:
        cp.start()

    for yy in range(4):
        for cp in a_dir(yy):
            cp.wait_recv()
    for cp in a_sum:
        cp.wait_recv()
    for yy in range(4):
        s = own[xl, yy, xh, 0:8] + fl[yy].astype(F32) + fr[yy].astype(F32)
        a1[yy] = s
        a1b[yy] = s.astype(BF)
    for hh in range(2):
        for cp in b_dir(hh):
            cp.wait_recv()
    for cp in b_sum:
        cp.wait_recv()
    for l_ in range(2):
        for hh in range(2):
            s = own[l_, y, hh, 8:16] + fd[l_, hh].astype(F32) + fu[l_, hh].astype(F32)
            b1[hh * 2 + l_] = s
            b1b[hh * 2 + l_] = s.astype(BF)

    second = []
    for d in range(3):
        second.append(
            pltpu.make_async_remote_copy(
                src_ref=a1b.at[(y + d + 1) % 4], dst_ref=ra2.at[d],
                send_sem=a2send.at[d], recv_sem=a2recv.at[d],
                device_id=y_dev[d], device_id_type=MESH,
            )
        )
        second.append(
            pltpu.make_async_remote_copy(
                src_ref=b1b.at[(x + d + 1) % 4], dst_ref=rb2.at[d],
                send_sem=b2send.at[d], recv_sem=b2recv.at[d],
                device_id=x_dev[d], device_id_type=MESH,
            )
        )
    for cp in second:
        cp.start()
    met(2)
    sent = list(a_sum) + list(b_sum)
    for k in range(4):
        sent += list(a_dir(k)) + list(a_rel(k))
    for k in range(2):
        sent += list(b_dir(k)) + list(b_rel(k))
    for cp in sent:
        cp.wait_send()
    for cp in second:
        cp.wait()
    sa = a1[y]
    sbb = b1[x]
    for d in range(3):
        sa = sa + ra2[d].astype(F32)
        sbb = sbb + rb2[d].astype(F32)
    tb[0:128] = sa.reshape(128, 128).astype(BF)
    tb[128:256] = sbb.reshape(128, 128).astype(BF)

    zb[...] = (
        jnp.dot(turnv[...], tb[...], preferred_element_type=F32).astype(BF).reshape(16, 16, 128)
    )
    z_copies = []
    for d in range(15):
        cp = pltpu.make_async_remote_copy(
            src_ref=zb.at[(z + d + 1) % 16], dst_ref=rz.at[d],
            send_sem=zsend.at[d], recv_sem=zrecv.at[d],
            device_id=z_dev[d], device_id_type=MESH,
        )
        z_copies.append(cp)
    for d in (7, 6, 8, 5, 9, 4, 10, 3, 11, 2, 12, 1, 13, 0, 14):
        z_copies[d].start()

    for cp in g_copies:
        cp.wait()
    build_shifts(ghalo, even, odd, w, n)
    pre[...] = jnp.zeros((512, C), F32)
    for t in range(27):
        a, b, c = t // 9, (t // 3) % 3, t % 3
        pre[...] += jnp.dot(
            tap_rows(even, odd, 2 - a, 2 - b, 2 - c),
            wv[:, C * t : C * t + C],
            preferred_element_type=F32,
        )
    for xx in range(8):
        rows = slice(64 * xx, 64 * xx + 64)
        gin_ref[xx] = (pre[rows, :] * live[rows, :]).reshape(8, 8, C).astype(BF)

    total = zb[z].astype(F32)
    for d in range(15):
        z_copies[d].wait()
        total = total + rz[d].astype(F32)
    fin[...] = total * (1.0 / 512.0)

    g_all = []
    for d in range(7):
        cp = pltpu.make_async_remote_copy(
            src_ref=fin, dst_ref=ag.at[n],
            send_sem=gsnd.at[d], recv_sem=grcv.at[d],
            device_id=n_dev[d], device_id_type=MESH,
        )
        cp.start()
        g_all.append(cp)
    ag[n] = fin[...]
    for cp in g_all:
        cp.wait()


def finish(act_in, gin_in, ag_in, act_out, gin_out, gw_out, ag, gw, sem):
    copies = [
        pltpu.make_async_copy(ag_in, ag, sem.at[0]),
        pltpu.make_async_copy(act_in, act_out, sem.at[1]),
        pltpu.make_async_copy(gin_in, gin_out, sem.at[2]),
    ]
    for cp in copies:
        cp.start()
    copies[0].wait()
    for m_ in range(8):
        for k in range(3):
            for t in range(5):
                lo = (5 * m_ + t) * 128
                gw[k : k + 1, lo : lo + 128] = ag[m_, 5 * k + t : 5 * k + t + 1, :]
    for k in range(3):
        gw[k : k + 1, 5120:5184] = ag[k, 15:16, 0:64]
    cp = pltpu.make_async_copy(gw, gw_out, sem.at[3])
    cp.start()
    copies[1].wait()
    copies[2].wait()
    cp.wait()


def local(features, weight, voxel_mask, cotangent):
    dma = pltpu.SemaphoreType.DMA
    vmem = pltpu.VMEM
    scratch = [
        vmem((C, 27 * C), BF),
        vmem((8, 8, 8), jnp.int32),
        vmem((8, 8, 8, C), BF),
        vmem((10, 10, 8, C), BF),
        vmem((10, 10, 8, C), BF),
        vmem((3, 10, 80, C), BF),
        vmem((3, 10, 64, C), BF),
        vmem((512, 5248), BF),
        vmem((512, C), F32),
        vmem((512, C), F32),
        vmem((512, C), BF),
        vmem((C, 512), BF),
        vmem((2, 4, 2, 16, 16, 128), F32),
        vmem((2, 4, 2, 16, 16, 128), BF),
        vmem((2, 4, 2, 16, 16, 128), BF),
        vmem((2, 4, 2, 16, 16, 128), BF),
        vmem((4, 8, 16, 128), F32),
        vmem((4, 8, 16, 128), F32),
        vmem((4, 8, 16, 128), BF),
        vmem((4, 8, 16, 128), BF),
        vmem((256, 128), BF),
        vmem((16, 16, 128), BF),
        vmem((16, 128), F32),
        vmem((4, 8, 16, 128), BF), vmem((4, 8, 16, 128), BF),
        vmem((2, 2, 8, 16, 128), BF), vmem((2, 2, 8, 16, 128), BF),
        vmem((4, 4, 16, 128), BF), vmem((4, 4, 16, 128), BF),
        vmem((2, 2, 4, 16, 128), BF), vmem((2, 2, 4, 16, 128), BF),
        vmem((3, 8, 16, 128), BF),
        vmem((3, 8, 16, 128), BF),
        vmem((15, 16, 128), BF),
        vmem((C, C), BF), vmem((256, 256), BF),
        dma((4,)),
        dma((8,)), dma((8,)), dma((8,)), dma((8,)),
        dma((8,)), dma((8,)),
        dma((2, 4)), dma((2, 4)), dma((2, 4)), dma((2, 4)), dma((2,)), dma((2,)),
        dma((2, 2)), dma((2, 2)), dma((2, 2)), dma((2, 2)), dma((2,)), dma((2,)),
        dma((3,)), dma((3,)), dma((3,)), dma((3,)),
        dma((15,)), dma((15,)),
        dma((7,)), dma((7,)),
        pltpu.SemaphoreType.REGULAR((3,)),
    ]
    any_ = pl.BlockSpec(memory_space=pl.ANY)
    hbm = pl.BlockSpec(memory_space=pltpu.HBM)
    vm = pl.BlockSpec(memory_space=pltpu.VMEM)
    act, gin, blocks = pl.pallas_call(
        kernel,
        name="sparse_conv",
        out_shape=(
            pltpu.VMEM((8, 8, 8, C), BF),
            pltpu.VMEM((8, 8, 8, C), BF),
            pltpu.VMEM((8, 16, 128), F32),
        ),
        in_specs=[hbm] * 4,
        out_specs=(vm, vm, vm),
        scratch_shapes=scratch,
        compiler_params=pltpu.CompilerParams(
            collective_id=0, has_side_effects=True, vmem_limit_bytes=61 * 1024 * 1024
        ),
    )(features, weight.T, voxel_mask, cotangent)
    return pl.pallas_call(
        finish,
        name="finish",
        out_shape=(
            jax.ShapeDtypeStruct((8, 8, 8, C), BF),
            jax.ShapeDtypeStruct((8, 8, 8, C), BF),
            jax.ShapeDtypeStruct((3, 27 * C), F32),
        ),
        in_specs=[any_] * 3,
        out_specs=(any_, any_, any_),
        scratch_shapes=[vmem((8, 16, 128), F32), vmem((3, 27 * C), F32), dma((4,))],
        compiler_params=pltpu.CompilerParams(vmem_limit_bytes=4 * 1024 * 1024),
    )(act, gin, blocks)


def solution(mesh):
    return jax.shard_map(
        local,
        mesh=mesh,
        in_specs=(
            P("wide", "narrow", None, None),
            P(),
            P("wide", "narrow", None),
            P("wide", "narrow", None, None),
        ),
        out_specs=(
            P("wide", "narrow", None, None),
            P("wide", "narrow", None, None),
            P("wide", None),
        ),
        check_vma=False,
    )
```

```python
import jax
import jax.numpy as jnp
from jax import lax
from jax.experimental import pallas as pl
from jax.experimental.pallas import tpu as pltpu
from jax.sharding import PartitionSpec as P

C = 192
BF = jnp.bfloat16
F32 = jnp.float32
MESH = pl.DeviceIdType.MESH
WIDE, NARROW = 64, 8
LAG = 3


def iota(shape, dim):
    return lax.broadcasted_iota(jnp.int32, shape, dim)


def build_shifts(src, even, odd, w, n):
    def body(x, carry):
        v = src[x].astype(F32)
        yy = iota((10, 8, C), 0)
        zz = iota((10, 8, C), 1)
        x_ok = jnp.logical_and(
            jnp.logical_or(x > 0, w > 0), jnp.logical_or(x < 9, w < WIDE - 1)
        )
        lo = jnp.where(n > 0, 0, 1)
        hi = jnp.where(n < NARROW - 1, 9, 8)
        lo = jnp.where(x_ok, lo, 100)
        v = jnp.where((yy >= lo) & (yy <= hi), v, 0.0)
        for c in range(3):
            if c == 0:
                s = jnp.where(zz == 0, 0.0, pltpu.roll(v, 1, 1))
            elif c == 1:
                s = v
            else:
                s = jnp.where(zz == 7, 0.0, pltpu.roll(v, 7, 1))
            s = s.reshape(80, C)
            even[c, x] = s.astype(BF)
            odd[c, x] = s[8:72].astype(BF)
        return carry

    lax.fori_loop(0, 10, body, 0)


def tap_rows(even, odd, a, b, c):
    if b == 1:
        v = odd[c, a : a + 8]
    else:
        v = even[c, a : a + 8, 8 * b : 8 * b + 64, :]
    return v.reshape(512, C)


def kernel(
    feat_hbm, w_hbm, mask_hbm, cot_hbm,
    act_ref, gin_ref, ag,
    wv, mask, cot, halo, ghalo, even, odd, cols, pre, live, gp2, gpt,
    own, sb, rb, s1b, a1, b1, a1b, b1b, tb, zb, fin,
    fl, fr, fd, fu, rpa, rma, rpb, rmb, ra2, rb2, rz, permv, turnv,
    lsem, hsend, hrecv, gsend, grecv, csend, crecv,
    ads, adr, ars, arr, ass, asr, bds, bdr, brs, brr, bss, bsr, a2send, a2recv, b2send, b2recv,
    zsend, zrecv, gsnd, grcv, ring,
):
    w = lax.axis_index("wide")
    n = lax.axis_index("narrow")
    core = w % 2
    xl = (w // 2) % 2
    z = w // 4
    y = n // 2
    xh = n % 2
    x = xh * 2 + xl

    def dev(z_, x_, c_, y_):
        return {"wide": (z_ * 2 + x_ % 2) * 2 + c_, "narrow": y_ * 2 + x_ // 2}

    near = []
    for dw, dn in ((1, 1), (1, -1), (-1, 1), (-1, -1), (0, 1), (0, -1), (1, 0), (-1, 0)):
        near.append(
            (dw, dn, {"wide": (w + dw + WIDE) % WIDE, "narrow": (n + dn + NARROW) % NARROW})
        )
    x_dev = [dev(z, (x + d) % 4, core, y) for d in (1, 2, 3)]
    y_dev = [dev(z, x, core, (y + d) % 4) for d in (1, 2, 3)]
    z_dev = [dev((z + d) % 16, x, core, y) for d in range(1, 16)]
    n_dev = [{"wide": w, "narrow": (n + d) % 8} for d in range(1, 8)]

    barrier = pltpu.get_barrier_semaphore()
    partners = [t[2] for t in near] + n_dev + x_dev + [z_dev[0], z_dev[14]]
    for p in partners:
        pl.semaphore_signal(barrier, inc=1, device_id=p, device_id_type=MESH)

    c_feat = pltpu.make_async_copy(feat_hbm, halo.at[1:9, 1:9], lsem.at[0])
    c_w = pltpu.make_async_copy(w_hbm, wv, lsem.at[1])
    c_cot = pltpu.make_async_copy(cot_hbm, cot, lsem.at[2])
    c_mask = pltpu.make_async_copy(mask_hbm, mask, lsem.at[3])
    c_mask.start()
    c_feat.start()
    c_w.start()
    c_cot.start()

    c_mask.wait()
    m = mask[...].astype(F32).reshape(64, 8).astype(BF)
    pick = (iota((512, 64), 0) // 8 == iota((512, 64), 1)).astype(F32).astype(BF)
    mm = jnp.dot(pick, m, preferred_element_type=F32)
    mm = jnp.where(iota((512, 8), 0) % 8 == iota((512, 8), 1), mm, 0.0).astype(BF)
    live[...] = jnp.dot(mm, jnp.ones((8, C), BF), preferred_element_type=F32)

    c_feat.wait()
    for xx in range(8):
        v = halo[1 + xx, 1:9].astype(F32) * live[64 * xx : 64 * xx + 64, :].reshape(8, 8, C)
        halo[1 + xx, 1:9] = v.astype(BF)

    pl.semaphore_wait(barrier, len(partners))

    def tell(d, k):
        for p in (z_dev[d - 1], z_dev[15 - d]):
            pl.semaphore_signal(ring.at[k], inc=1, device_id=p, device_id_type=MESH)

    def met(k):
        pl.semaphore_wait(ring.at[k], 2)

    tell(1, 0)

    def exchange(buf, send, recv):
        copies = []
        for k, (dw, dn, d) in enumerate(near):
            sx = {1: slice(8, 9), -1: slice(1, 2), 0: slice(1, 9)}[dw]
            tx = {1: slice(0, 1), -1: slice(9, 10), 0: slice(1, 9)}[dw]
            sy = {1: slice(8, 9), -1: slice(1, 2), 0: slice(1, 9)}[dn]
            ty = {1: slice(0, 1), -1: slice(9, 10), 0: slice(1, 9)}[dn]
            cp = pltpu.make_async_remote_copy(
                src_ref=buf.at[sx, sy],
                dst_ref=buf.at[tx, ty],
                send_sem=send.at[k],
                recv_sem=recv.at[k],
                device_id=d,
                device_id_type=MESH,
            )
            cp.start()
            copies.append(cp)
        return copies

    halo_copies = exchange(halo, hsend, hrecv)
    cols[:, 5120:5248] = jnp.zeros((512, 128), BF)
    r = iota((C, C), 0)
    q = (r >= 96).astype(jnp.int32)
    r = r - 96 * q
    rl = (r >= 48).astype(jnp.int32)
    r = r - 48 * rl
    rk = (r >= 16).astype(jnp.int32) + (r >= 32).astype(jnp.int32)
    rz_ = r - 16 * rk
    rc = jnp.where(q == 1, core, 1 - core)
    rj = 3 * ((rz_ * 2 + rl) * 2 + rc) + rk
    permv[...] = (rj == iota((C, C), 1)).astype(F32).astype(BF)
    rr = iota((256, 256), 0)
    turnv[...] = (iota((256, 256), 1) == (rr % 16) * 16 + rr // 16).astype(F32).astype(BF)

    for cp in halo_copies:
        cp.wait()
    met(0)
    tell(2, 1)

    build_shifts(halo, even, odd, w, n)
    for t in range(27):
        a, b, c = t // 9, (t // 3) % 3, t % 3
        cols[:, C * t : C * t + C] = tap_rows(even, odd, a, b, c)

    c_w.wait()
    pre[...] = lax.dot_general(
        cols[:, 0:5184], wv[...], (((1,), (1,)), ((), ())), preferred_element_type=F32
    )

    met(1)
    tell(4, 2)
    c_cot.wait()
    for xx in range(8):
        rows = slice(64 * xx, 64 * xx + 64)
        pv = pre[rows, :]
        lv = live[rows, :]
        sig = jax.nn.sigmoid(pv)
        act_ref[xx] = (pv * sig * lv).reshape(8, 8, C).astype(BF)
        slope = sig * (1.0 + pv * (1.0 - sig))
        ct = cot[xx].astype(F32).reshape(64, C)
        g = ct * lv * slope
        gp2[rows, :] = g.astype(BF)
        ghalo[1 + xx, 1:9] = g.reshape(8, 8, C).astype(BF)

    g_copies = exchange(ghalo, gsend, grecv)

    gpt[...] = lax.dot_general(
        permv[...], gp2[...], (((1,), (1,)), ((), ())), preferred_element_type=F32
    ).astype(BF)

    tail = jnp.dot(gpt[...], cols[:, 5120:5248], preferred_element_type=F32)
    for l_ in range(2):
        for m_ in range(8):
            k = m_ % 3
            lo = 48 * l_ + 16 * k
            sb[l_, m_ // 2, m_ % 2, 15] = tail[lo : lo + 16].astype(BF)
            own[l_, m_ // 2, m_ % 2, 15] = tail[96 + lo : 112 + lo]

    def owner(i):
        k = i % 4
        dy = jnp.where(k == 0, 2, jnp.where(k == 1, 1, jnp.where(k == 2, 3, 0)))
        return (y + dy) % 4, (xh + 1 + i // 4) % 2

    partner = dev(z, x, 1 - core, y)

    def core_copy(i):
        yy, hh = owner(i)
        return pltpu.make_async_remote_copy(
            src_ref=sb.at[:, yy, hh],
            dst_ref=rb.at[:, yy, hh],
            send_sem=csend.at[i],
            recv_sem=crecv.at[i],
            device_id=partner,
            device_id_type=MESH,
        )

    def wgrad(i, carry):
        yy, hh = owner(i)
        col = pl.multiple_of((yy * 2 + hh) * 640, 128)
        o = jnp.dot(gpt[...], cols[:, pl.ds(col, 640)], preferred_element_type=F32)
        for l_ in range(2):
            for k in range(3):
                lo = 48 * l_ + 16 * k
                for t in range(5):
                    sb[l_, yy, hh, 5 * k + t] = o[lo : lo + 16, 128 * t : 128 * t + 128].astype(BF)
                    own[l_, yy, hh, 5 * k + t] = o[96 + lo : 112 + lo, 128 * t : 128 * t + 128]
        core_copy(i).start()
        return carry

    xp, xo, xm = (x + 1) % 4, (x + 2) % 4, (x + 3) % 4
    yp, yo, ym = (y + 1) % 4, (y + 2) % 4, (y + 3) % 4

    def remote(src, dst, send, recv, d):
        return pltpu.make_async_remote_copy(
            src_ref=src, dst_ref=dst, send_sem=send, recv_sem=recv,
            device_id=d, device_id_type=MESH,
        )

    def a_part(xt, yy, lo):
        return s1b.at[xt % 2, yy, xt // 2, pl.ds(lo, 4)]

    def a_dir(yy):
        return (
            remote(a_part(xp, yy, 4), fl.at[yy, pl.ds(4, 4)], ads.at[0, yy], adr.at[0, yy], x_dev[0]),
            remote(a_part(xm, yy, 0), fr.at[yy, pl.ds(0, 4)], ads.at[1, yy], adr.at[1, yy], x_dev[2]),
        )

    def a_rel(yy):
        return (
            remote(a_part(xo, yy, 0), rpa.at[yy], ars.at[0, yy], arr.at[0, yy], x_dev[0]),
            remote(a_part(xo, yy, 4), rma.at[yy], ars.at[1, yy], arr.at[1, yy], x_dev[2]),
        )

    def b_part(yt, hh, lo):
        return s1b.at[:, yt, hh, pl.ds(lo, 4)]

    def b_dir(hh):
        return (
            remote(b_part(yp, hh, 12), fd.at[:, hh, pl.ds(4, 4)], bds.at[0, hh], bdr.at[0, hh], y_dev[0]),
            remote(b_part(ym, hh, 8), fu.at[:, hh, pl.ds(0, 4)], bds.at[1, hh], bdr.at[1, hh], y_dev[2]),
        )

    def b_rel(hh):
        return (
            remote(b_part(yo, hh, 8), rpb.at[hh], brs.at[0, hh], brr.at[0, hh], y_dev[0]),
            remote(b_part(yo, hh, 12), rmb.at[hh], brs.at[1, hh], brr.at[1, hh], y_dev[2]),
        )

    def a_sum(yy):
        return (
            remote(a_part(xp, yy, 0), fl.at[yy, pl.ds(0, 4)], ass.at[0, yy], asr.at[0, yy], x_dev[0]),
            remote(a_part(xm, yy, 4), fr.at[yy, pl.ds(4, 4)], ass.at[1, yy], asr.at[1, yy], x_dev[2]),
        )

    def b_sum(hh):
        return (
            remote(b_part(yp, hh, 8), fd.at[:, hh, pl.ds(0, 4)], bss.at[0, hh], bsr.at[0, hh], y_dev[0]),
            remote(b_part(ym, hh, 12), fu.at[:, hh, pl.ds(4, 4)], bss.at[1, hh], bsr.at[1, hh], y_dev[2]),
        )

    def a_forward(yy):
        for cp in a_rel(yy):
            cp.wait_recv()
        s = own[xp % 2, yy, xp // 2, 0:4] + rpa[yy].astype(F32)
        s1b[xp % 2, yy, xp // 2, 0:4] = s.astype(BF)
        s = own[xm % 2, yy, xm // 2, 4:8] + rma[yy].astype(F32)
        s1b[xm % 2, yy, xm // 2, 4:8] = s.astype(BF)
        for cp in a_sum(yy):
            cp.start()

    def b_forward(hh):
        for cp in b_rel(hh):
            cp.wait_recv()
        for l_ in range(2):
            s = own[l_, yp, hh, 8:12] + rpb[hh, l_].astype(F32)
            s1b[l_, yp, hh, 8:12] = s.astype(BF)
            s = own[l_, ym, hh, 12:16] + rmb[hh, l_].astype(F32)
            s1b[l_, ym, hh, 12:16] = s.astype(BF)
        for cp in b_sum(hh):
            cp.start()

    def first(i, carry):
        yy, hh = owner(i)
        core_copy(i).wait()
        for l_ in range(2):
            s = own[l_, yy, hh] + rb[l_, yy, hh].astype(F32)
            own[l_, yy, hh] = s
            s1b[l_, yy, hh] = s.astype(BF)
        for l_ in range(2):
            xt = hh * 2 + l_
            pl.when(xt == xo)(lambda: [cp.start() for cp in a_rel(yy)] and None)
            pl.when(xt == xp)(a_dir(yy)[0].start)
            pl.when(xt == xm)(a_dir(yy)[1].start)
        pl.when(yy == yo)(lambda: [cp.start() for cp in b_rel(hh)] and None)
        pl.when(yy == yp)(b_dir(hh)[0].start)
        pl.when(yy == ym)(b_dir(hh)[1].start)
        pl.when(i >= 4)(lambda: a_forward(yy))
        pl.when(i == 3)(lambda: b_forward((xh + 1) % 2))
        pl.when(i == 7)(lambda: b_forward(xh))
        return carry

    def both(i, carry):
        wgrad(i, carry)
        first(i - LAG, carry)
        return carry

    lax.fori_loop(0, LAG, wgrad, 0)
    lax.fori_loop(LAG, 8, both, 0)
    lax.fori_loop(8 - LAG, 8, first, 0)
    for yy in range(4):
        for cp in a_dir(yy) + a_sum(yy):
            cp.wait_recv()
    for yy in range(4):
        s = own[xl, yy, xh, 0:8] + fl[yy].astype(F32) + fr[yy].astype(F32)
        a1[yy] = s
        a1b[yy] = s.astype(BF)
    for hh in range(2):
        for cp in b_dir(hh) + b_sum(hh):
            cp.wait_recv()
    for l_ in range(2):
        for hh in range(2):
            s = own[l_, y, hh, 8:16] + fd[l_, hh].astype(F32) + fu[l_, hh].astype(F32)
            b1[hh * 2 + l_] = s
            b1b[hh * 2 + l_] = s.astype(BF)

    second = []
    for d in (1, 0, 2):
        second.append(
            pltpu.make_async_remote_copy(
                src_ref=a1b.at[(y + d + 1) % 4], dst_ref=ra2.at[d],
                send_sem=a2send.at[d], recv_sem=a2recv.at[d],
                device_id=y_dev[d], device_id_type=MESH,
            )
        )
        second.append(
            pltpu.make_async_remote_copy(
                src_ref=b1b.at[(x + d + 1) % 4], dst_ref=rb2.at[d],
                send_sem=b2send.at[d], recv_sem=b2recv.at[d],
                device_id=x_dev[d], device_id_type=MESH,
            )
        )
    for cp in second:
        cp.start()
    met(2)
    sent = []
    for k in range(4):
        sent += a_dir(k) + a_rel(k) + a_sum(k)
    for k in range(2):
        sent += b_dir(k) + b_rel(k) + b_sum(k)
    for cp in sent:
        cp.wait_send()
    for cp in second:
        cp.wait()
    sa = a1[y]
    sbb = b1[x]
    for d in range(3):
        sa = sa + ra2[d].astype(F32)
        sbb = sbb + rb2[d].astype(F32)
    tb[0:128] = sa.reshape(128, 128).astype(BF)
    tb[128:256] = sbb.reshape(128, 128).astype(BF)

    zb[...] = (
        jnp.dot(turnv[...], tb[...], preferred_element_type=F32).astype(BF).reshape(16, 16, 128)
    )
    z_copies = []
    for d in range(15):
        cp = pltpu.make_async_remote_copy(
            src_ref=zb.at[(z + d + 1) % 16], dst_ref=rz.at[d],
            send_sem=zsend.at[d], recv_sem=zrecv.at[d],
            device_id=z_dev[d], device_id_type=MESH,
        )
        z_copies.append(cp)
    for d in (7, 6, 8, 5, 9, 4, 10, 3, 11, 2, 12, 1, 13, 0, 14):
        z_copies[d].start()

    for cp in g_copies:
        cp.wait()
    build_shifts(ghalo, even, odd, w, n)
    pre[...] = jnp.zeros((512, C), F32)
    for t in range(27):
        a, b, c = t // 9, (t // 3) % 3, t % 3
        pre[...] += jnp.dot(
            tap_rows(even, odd, 2 - a, 2 - b, 2 - c),
            wv[:, C * t : C * t + C],
            preferred_element_type=F32,
        )
    for xx in range(8):
        rows = slice(64 * xx, 64 * xx + 64)
        gin_ref[xx] = (pre[rows, :] * live[rows, :]).reshape(8, 8, C).astype(BF)

    total = zb[z].astype(F32)
    for d in range(15):
        z_copies[d].wait()
        total = total + rz[d].astype(F32)
    fin[...] = total * (1.0 / 512.0)

    g_all = []
    for d in (2, 4, 3, 0, 6, 1, 5):
        cp = pltpu.make_async_remote_copy(
            src_ref=fin, dst_ref=ag.at[n],
            send_sem=gsnd.at[d], recv_sem=grcv.at[d],
            device_id=n_dev[d], device_id_type=MESH,
        )
        cp.start()
        g_all.append(cp)
    ag[n] = fin[...]
    for cp in g_all:
        cp.wait()


def finish(act_in, gin_in, ag_in, act_out, gin_out, gw_out, ag, gw, sem):
    copies = [
        pltpu.make_async_copy(ag_in, ag, sem.at[0]),
        pltpu.make_async_copy(act_in, act_out, sem.at[1]),
        pltpu.make_async_copy(gin_in, gin_out, sem.at[2]),
    ]
    for cp in copies:
        cp.start()
    copies[0].wait()
    for m_ in range(8):
        for k in range(3):
            for t in range(5):
                lo = (5 * m_ + t) * 128
                gw[k : k + 1, lo : lo + 128] = ag[m_, 5 * k + t : 5 * k + t + 1, :]
    for k in range(3):
        gw[k : k + 1, 5120:5184] = ag[k, 15:16, 0:64]
    cp = pltpu.make_async_copy(gw, gw_out, sem.at[3])
    cp.start()
    copies[1].wait()
    copies[2].wait()
    cp.wait()


def local(features, weight, voxel_mask, cotangent):
    dma = pltpu.SemaphoreType.DMA
    vmem = pltpu.VMEM
    scratch = [
        vmem((C, 27 * C), BF),
        vmem((8, 8, 8), jnp.int32),
        vmem((8, 8, 8, C), BF),
        vmem((10, 10, 8, C), BF),
        vmem((10, 10, 8, C), BF),
        vmem((3, 10, 80, C), BF),
        vmem((3, 10, 64, C), BF),
        vmem((512, 5248), BF),
        vmem((512, C), F32),
        vmem((512, C), F32),
        vmem((512, C), BF),
        vmem((C, 512), BF),
        vmem((2, 4, 2, 16, 16, 128), F32),
        vmem((2, 4, 2, 16, 16, 128), BF),
        vmem((2, 4, 2, 16, 16, 128), BF),
        vmem((2, 4, 2, 16, 16, 128), BF),
        vmem((4, 8, 16, 128), F32),
        vmem((4, 8, 16, 128), F32),
        vmem((4, 8, 16, 128), BF),
        vmem((4, 8, 16, 128), BF),
        vmem((256, 128), BF),
        vmem((16, 16, 128), BF),
        vmem((16, 128), F32),
        vmem((4, 8, 16, 128), BF), vmem((4, 8, 16, 128), BF),
        vmem((2, 2, 8, 16, 128), BF), vmem((2, 2, 8, 16, 128), BF),
        vmem((4, 4, 16, 128), BF), vmem((4, 4, 16, 128), BF),
        vmem((2, 2, 4, 16, 128), BF), vmem((2, 2, 4, 16, 128), BF),
        vmem((3, 8, 16, 128), BF),
        vmem((3, 8, 16, 128), BF),
        vmem((15, 16, 128), BF),
        vmem((C, C), BF), vmem((256, 256), BF),
        dma((4,)),
        dma((8,)), dma((8,)), dma((8,)), dma((8,)),
        dma((8,)), dma((8,)),
        dma((2, 4)), dma((2, 4)), dma((2, 4)), dma((2, 4)), dma((2, 4)), dma((2, 4)),
        dma((2, 2)), dma((2, 2)), dma((2, 2)), dma((2, 2)), dma((2, 2)), dma((2, 2)),
        dma((3,)), dma((3,)), dma((3,)), dma((3,)),
        dma((15,)), dma((15,)),
        dma((7,)), dma((7,)),
        pltpu.SemaphoreType.REGULAR((3,)),
    ]
    any_ = pl.BlockSpec(memory_space=pl.ANY)
    hbm = pl.BlockSpec(memory_space=pltpu.HBM)
    vm = pl.BlockSpec(memory_space=pltpu.VMEM)
    act, gin, blocks = pl.pallas_call(
        kernel,
        name="sparse_conv",
        out_shape=(
            pltpu.VMEM((8, 8, 8, C), BF),
            pltpu.VMEM((8, 8, 8, C), BF),
            pltpu.VMEM((8, 16, 128), F32),
        ),
        in_specs=[hbm] * 4,
        out_specs=(vm, vm, vm),
        scratch_shapes=scratch,
        compiler_params=pltpu.CompilerParams(
            collective_id=0, has_side_effects=True, vmem_limit_bytes=61 * 1024 * 1024
        ),
    )(features, weight.T, voxel_mask, cotangent)
    return pl.pallas_call(
        finish,
        name="finish",
        out_shape=(
            jax.ShapeDtypeStruct((8, 8, 8, C), BF),
            jax.ShapeDtypeStruct((8, 8, 8, C), BF),
            jax.ShapeDtypeStruct((3, 27 * C), F32),
        ),
        in_specs=[any_] * 3,
        out_specs=(any_, any_, any_),
        scratch_shapes=[vmem((8, 16, 128), F32), vmem((3, 27 * C), F32), dma((4,))],
        compiler_params=pltpu.CompilerParams(vmem_limit_bytes=4 * 1024 * 1024),
    )(act, gin, blocks)


def solution(mesh):
    return jax.shard_map(
        local,
        mesh=mesh,
        in_specs=(
            P("wide", "narrow", None, None),
            P(),
            P("wide", "narrow", None),
            P("wide", "narrow", None, None),
        ),
        out_specs=(
            P("wide", "narrow", None, None),
            P("wide", "narrow", None, None),
            P("wide", None),
        ),
        check_vma=False,
    )
```

```python
import jax
import jax.numpy as jnp
from jax import lax
from jax.experimental import pallas as pl
from jax.experimental.pallas import tpu as pltpu
from jax.sharding import PartitionSpec as P

C = 192
BF = jnp.bfloat16
F32 = jnp.float32
MESH = pl.DeviceIdType.MESH
WIDE, NARROW = 64, 8
LAG = 3


def iota(shape, dim):
    return lax.broadcasted_iota(jnp.int32, shape, dim)


def build_shifts(src, even, odd, w, n):
    def body(x, carry):
        v = src[x].astype(F32)
        yy = iota((10, 8, C), 0)
        zz = iota((10, 8, C), 1)
        x_ok = jnp.logical_and(
            jnp.logical_or(x > 0, w > 0), jnp.logical_or(x < 9, w < WIDE - 1)
        )
        lo = jnp.where(n > 0, 0, 1)
        hi = jnp.where(n < NARROW - 1, 9, 8)
        lo = jnp.where(x_ok, lo, 100)
        v = jnp.where((yy >= lo) & (yy <= hi), v, 0.0)
        for c in range(3):
            if c == 0:
                s = jnp.where(zz == 0, 0.0, pltpu.roll(v, 1, 1))
            elif c == 1:
                s = v
            else:
                s = jnp.where(zz == 7, 0.0, pltpu.roll(v, 7, 1))
            s = s.reshape(80, C)
            even[c, x] = s.astype(BF)
            odd[c, x] = s[8:72].astype(BF)
        return carry

    lax.fori_loop(0, 10, body, 0)


def tap_rows(even, odd, a, b, c):
    if b == 1:
        v = odd[c, a : a + 8]
    else:
        v = even[c, a : a + 8, 8 * b : 8 * b + 64, :]
    return v.reshape(512, C)


def kernel(
    feat_hbm, w_hbm, mask_hbm, cot_hbm,
    act_ref, gin_ref, ag,
    wv, mask, cot, halo, ghalo, even, odd, cols, pre, live, gp2, gpt,
    own, sb, rb, s1b, a1, b1, a1b, b1b, tb, zb, fin,
    fl, fr, fd, fu, rpa, rma, rpb, rmb, ra2, rb2, rz, permv, turnv,
    lsem, hsend, hrecv, gsend, grecv, csend, crecv,
    ads, adr, ars, arr, ass, asr, bds, bdr, brs, brr, bss, bsr, a2send, a2recv, b2send, b2recv,
    zsend, zrecv, gsnd, grcv, ring,
):
    w = lax.axis_index("wide")
    n = lax.axis_index("narrow")
    core = w % 2
    xl = (w // 2) % 2
    z = w // 4
    y = n // 2
    xh = n % 2
    x = xh * 2 + xl

    def dev(z_, x_, c_, y_):
        return {"wide": (z_ * 2 + x_ % 2) * 2 + c_, "narrow": y_ * 2 + x_ // 2}

    near = []
    for dw, dn in ((1, 1), (1, -1), (-1, 1), (-1, -1), (0, 1), (0, -1), (1, 0), (-1, 0)):
        near.append(
            (dw, dn, {"wide": (w + dw + WIDE) % WIDE, "narrow": (n + dn + NARROW) % NARROW})
        )
    x_dev = [dev(z, (x + d) % 4, core, y) for d in (1, 2, 3)]
    y_dev = [dev(z, x, core, (y + d) % 4) for d in (1, 2, 3)]
    z_dev = [dev((z + d) % 16, x, core, y) for d in range(1, 16)]
    n_dev = [{"wide": w, "narrow": (n + d) % 8} for d in range(1, 8)]

    barrier = pltpu.get_barrier_semaphore()
    partners = [t[2] for t in near] + n_dev + x_dev + [z_dev[0], z_dev[14]]
    for p in partners:
        pl.semaphore_signal(barrier, inc=1, device_id=p, device_id_type=MESH)

    c_feat = pltpu.make_async_copy(feat_hbm, halo.at[1:9, 1:9], lsem.at[0])
    c_w = pltpu.make_async_copy(w_hbm, wv, lsem.at[1])
    c_cot = pltpu.make_async_copy(cot_hbm, cot, lsem.at[2])
    c_mask = pltpu.make_async_copy(mask_hbm, mask, lsem.at[3])
    c_mask.start()
    c_feat.start()
    c_w.start()
    c_cot.start()

    c_mask.wait()
    m = mask[...].astype(F32).reshape(64, 8).astype(BF)
    pick = (iota((512, 64), 0) // 8 == iota((512, 64), 1)).astype(F32).astype(BF)
    mm = jnp.dot(pick, m, preferred_element_type=F32)
    mm = jnp.where(iota((512, 8), 0) % 8 == iota((512, 8), 1), mm, 0.0).astype(BF)
    live[...] = jnp.dot(mm, jnp.ones((8, C), BF), preferred_element_type=F32)

    c_feat.wait()
    for xx in range(8):
        v = halo[1 + xx, 1:9].astype(F32) * live[64 * xx : 64 * xx + 64, :].reshape(8, 8, C)
        halo[1 + xx, 1:9] = v.astype(BF)

    pl.semaphore_wait(barrier, len(partners))

    def tell(d, k):
        for p in (z_dev[d - 1], z_dev[15 - d]):
            pl.semaphore_signal(ring.at[k], inc=1, device_id=p, device_id_type=MESH)

    def met(k):
        pl.semaphore_wait(ring.at[k], 2)

    tell(1, 0)

    def exchange(buf, send, recv):
        copies = []
        for k, (dw, dn, d) in enumerate(near):
            sx = {1: slice(8, 9), -1: slice(1, 2), 0: slice(1, 9)}[dw]
            tx = {1: slice(0, 1), -1: slice(9, 10), 0: slice(1, 9)}[dw]
            sy = {1: slice(8, 9), -1: slice(1, 2), 0: slice(1, 9)}[dn]
            ty = {1: slice(0, 1), -1: slice(9, 10), 0: slice(1, 9)}[dn]
            cp = pltpu.make_async_remote_copy(
                src_ref=buf.at[sx, sy],
                dst_ref=buf.at[tx, ty],
                send_sem=send.at[k],
                recv_sem=recv.at[k],
                device_id=d,
                device_id_type=MESH,
            )
            cp.start()
            copies.append(cp)
        return copies

    halo_copies = exchange(halo, hsend, hrecv)
    cols[:, 5120:5248] = jnp.zeros((512, 128), BF)
    r = iota((C, C), 0)
    q = (r >= 96).astype(jnp.int32)
    r = r - 96 * q
    rl = (r >= 48).astype(jnp.int32)
    r = r - 48 * rl
    rk = (r >= 16).astype(jnp.int32) + (r >= 32).astype(jnp.int32)
    rz_ = r - 16 * rk
    rc = jnp.where(q == 1, core, 1 - core)
    rj = 3 * ((rz_ * 2 + rl) * 2 + rc) + rk
    permv[...] = (rj == iota((C, C), 1)).astype(F32).astype(BF)
    rr = iota((256, 256), 0)
    turnv[...] = (iota((256, 256), 1) == (rr % 16) * 16 + rr // 16).astype(F32).astype(BF)

    for cp in halo_copies:
        cp.wait()
    met(0)
    tell(2, 1)

    build_shifts(halo, even, odd, w, n)
    for t in range(27):
        a, b, c = t // 9, (t // 3) % 3, t % 3
        cols[:, C * t : C * t + C] = tap_rows(even, odd, a, b, c)

    c_w.wait()
    pre[...] = lax.dot_general(
        cols[:, 0:5184], wv[...], (((1,), (1,)), ((), ())), preferred_element_type=F32
    )

    met(1)
    tell(4, 2)
    c_cot.wait()
    for xx in range(8):
        rows = slice(64 * xx, 64 * xx + 64)
        pv = pre[rows, :]
        lv = live[rows, :]
        sig = jax.nn.sigmoid(pv)
        act_ref[xx] = (pv * sig * lv).reshape(8, 8, C).astype(BF)
        slope = sig * (1.0 + pv * (1.0 - sig))
        ct = cot[xx].astype(F32).reshape(64, C)
        g = ct * lv * slope
        gp2[rows, :] = g.astype(BF)
        ghalo[1 + xx, 1:9] = g.reshape(8, 8, C).astype(BF)


    gpt[...] = lax.dot_general(
        permv[...], gp2[...], (((1,), (1,)), ((), ())), preferred_element_type=F32
    ).astype(BF)

    tail = jnp.dot(gpt[...], cols[:, 5120:5248], preferred_element_type=F32)
    for l_ in range(2):
        for m_ in range(8):
            k = m_ % 3
            lo = 48 * l_ + 16 * k
            sb[l_, m_ // 2, m_ % 2, 15] = tail[lo : lo + 16].astype(BF)
            own[l_, m_ // 2, m_ % 2, 15] = tail[96 + lo : 112 + lo]

    def owner(i):
        k = i % 4
        dy = jnp.where(k == 0, 2, jnp.where(k == 1, 1, jnp.where(k == 2, 3, 0)))
        return (y + dy) % 4, (xh + 1 + i // 4) % 2

    partner = dev(z, x, 1 - core, y)

    def core_copy(i):
        yy, hh = owner(i)
        return pltpu.make_async_remote_copy(
            src_ref=sb.at[:, yy, hh],
            dst_ref=rb.at[:, yy, hh],
            send_sem=csend.at[i],
            recv_sem=crecv.at[i],
            device_id=partner,
            device_id_type=MESH,
        )

    def wgrad(i, carry):
        yy, hh = owner(i)
        col = pl.multiple_of((yy * 2 + hh) * 640, 128)
        o = jnp.dot(gpt[...], cols[:, pl.ds(col, 640)], preferred_element_type=F32)
        for l_ in range(2):
            for k in range(3):
                lo = 48 * l_ + 16 * k
                for t in range(5):
                    sb[l_, yy, hh, 5 * k + t] = o[lo : lo + 16, 128 * t : 128 * t + 128].astype(BF)
                    own[l_, yy, hh, 5 * k + t] = o[96 + lo : 112 + lo, 128 * t : 128 * t + 128]
        core_copy(i).start()
        return carry

    xp, xo, xm = (x + 1) % 4, (x + 2) % 4, (x + 3) % 4
    yp, yo, ym = (y + 1) % 4, (y + 2) % 4, (y + 3) % 4

    def remote(src, dst, send, recv, d):
        return pltpu.make_async_remote_copy(
            src_ref=src, dst_ref=dst, send_sem=send, recv_sem=recv,
            device_id=d, device_id_type=MESH,
        )

    def a_part(xt, yy, lo):
        return s1b.at[xt % 2, yy, xt // 2, pl.ds(lo, 4)]

    def a_dir(yy):
        return (
            remote(a_part(xp, yy, 4), fl.at[yy, pl.ds(4, 4)], ads.at[0, yy], adr.at[0, yy], x_dev[0]),
            remote(a_part(xm, yy, 0), fr.at[yy, pl.ds(0, 4)], ads.at[1, yy], adr.at[1, yy], x_dev[2]),
        )

    def a_rel(yy):
        return (
            remote(a_part(xo, yy, 0), rpa.at[yy], ars.at[0, yy], arr.at[0, yy], x_dev[0]),
            remote(a_part(xo, yy, 4), rma.at[yy], ars.at[1, yy], arr.at[1, yy], x_dev[2]),
        )

    def b_part(yt, hh, lo):
        return s1b.at[:, yt, hh, pl.ds(lo, 4)]

    def b_dir(hh):
        return (
            remote(b_part(yp, hh, 12), fd.at[:, hh, pl.ds(4, 4)], bds.at[0, hh], bdr.at[0, hh], y_dev[0]),
            remote(b_part(ym, hh, 8), fu.at[:, hh, pl.ds(0, 4)], bds.at[1, hh], bdr.at[1, hh], y_dev[2]),
        )

    def b_rel(hh):
        return (
            remote(b_part(yo, hh, 8), rpb.at[hh], brs.at[0, hh], brr.at[0, hh], y_dev[0]),
            remote(b_part(yo, hh, 12), rmb.at[hh], brs.at[1, hh], brr.at[1, hh], y_dev[2]),
        )

    def a_sum(yy):
        return (
            remote(a_part(xp, yy, 0), fl.at[yy, pl.ds(0, 4)], ass.at[0, yy], asr.at[0, yy], x_dev[0]),
            remote(a_part(xm, yy, 4), fr.at[yy, pl.ds(4, 4)], ass.at[1, yy], asr.at[1, yy], x_dev[2]),
        )

    def b_sum(hh):
        return (
            remote(b_part(yp, hh, 8), fd.at[:, hh, pl.ds(0, 4)], bss.at[0, hh], bsr.at[0, hh], y_dev[0]),
            remote(b_part(ym, hh, 12), fu.at[:, hh, pl.ds(4, 4)], bss.at[1, hh], bsr.at[1, hh], y_dev[2]),
        )

    def a_forward(yy):
        for cp in a_rel(yy):
            cp.wait_recv()
        s = own[xp % 2, yy, xp // 2, 0:4] + rpa[yy].astype(F32)
        s1b[xp % 2, yy, xp // 2, 0:4] = s.astype(BF)
        s = own[xm % 2, yy, xm // 2, 4:8] + rma[yy].astype(F32)
        s1b[xm % 2, yy, xm // 2, 4:8] = s.astype(BF)
        for cp in a_sum(yy):
            cp.start()

    def b_forward(hh):
        for cp in b_rel(hh):
            cp.wait_recv()
        for l_ in range(2):
            s = own[l_, yp, hh, 8:12] + rpb[hh, l_].astype(F32)
            s1b[l_, yp, hh, 8:12] = s.astype(BF)
            s = own[l_, ym, hh, 12:16] + rmb[hh, l_].astype(F32)
            s1b[l_, ym, hh, 12:16] = s.astype(BF)
        for cp in b_sum(hh):
            cp.start()

    def first(i, carry):
        yy, hh = owner(i)
        core_copy(i).wait()
        for l_ in range(2):
            s = own[l_, yy, hh] + rb[l_, yy, hh].astype(F32)
            own[l_, yy, hh] = s
            s1b[l_, yy, hh] = s.astype(BF)
        for l_ in range(2):
            xt = hh * 2 + l_
            pl.when(xt == xo)(lambda: [cp.start() for cp in a_rel(yy)] and None)
            pl.when(xt == xp)(a_dir(yy)[0].start)
            pl.when(xt == xm)(a_dir(yy)[1].start)
        pl.when(yy == yo)(lambda: [cp.start() for cp in b_rel(hh)] and None)
        pl.when(yy == yp)(b_dir(hh)[0].start)
        pl.when(yy == ym)(b_dir(hh)[1].start)
        pl.when(i >= 4)(lambda: a_forward(yy))
        pl.when(i == 3)(lambda: b_forward((xh + 1) % 2))
        pl.when(i == 7)(lambda: b_forward(xh))
        return carry

    def both(i, carry):
        wgrad(i, carry)
        first(i - LAG, carry)
        return carry

    lax.fori_loop(0, LAG, wgrad, 0)
    lax.fori_loop(LAG, 8, both, 0)
    lax.fori_loop(8 - LAG, 8, first, 0)
    for yy in range(4):
        for cp in a_dir(yy) + a_sum(yy):
            cp.wait_recv()
    for yy in range(4):
        s = own[xl, yy, xh, 0:8] + fl[yy].astype(F32) + fr[yy].astype(F32)
        a1[yy] = s
        a1b[yy] = s.astype(BF)
    for hh in range(2):
        for cp in b_dir(hh) + b_sum(hh):
            cp.wait_recv()
    for l_ in range(2):
        for hh in range(2):
            s = own[l_, y, hh, 8:16] + fd[l_, hh].astype(F32) + fu[l_, hh].astype(F32)
            b1[hh * 2 + l_] = s
            b1b[hh * 2 + l_] = s.astype(BF)

    second = []
    for d in (1, 0, 2):
        second.append(
            pltpu.make_async_remote_copy(
                src_ref=a1b.at[(y + d + 1) % 4], dst_ref=ra2.at[d],
                send_sem=a2send.at[d], recv_sem=a2recv.at[d],
                device_id=y_dev[d], device_id_type=MESH,
            )
        )
        second.append(
            pltpu.make_async_remote_copy(
                src_ref=b1b.at[(x + d + 1) % 4], dst_ref=rb2.at[d],
                send_sem=b2send.at[d], recv_sem=b2recv.at[d],
                device_id=x_dev[d], device_id_type=MESH,
            )
        )
    for cp in second:
        cp.start()
    g_copies = exchange(ghalo, gsend, grecv)
    met(2)
    sent = []
    for k in range(4):
        sent += a_dir(k) + a_rel(k) + a_sum(k)
    for k in range(2):
        sent += b_dir(k) + b_rel(k) + b_sum(k)
    for cp in sent:
        cp.wait_send()
    for cp in second:
        cp.wait()
    sa = a1[y]
    sbb = b1[x]
    for d in range(3):
        sa = sa + ra2[d].astype(F32)
        sbb = sbb + rb2[d].astype(F32)
    tb[0:128] = sa.reshape(128, 128).astype(BF)
    tb[128:256] = sbb.reshape(128, 128).astype(BF)

    zb[...] = (
        jnp.dot(turnv[...], tb[...], preferred_element_type=F32).astype(BF).reshape(16, 16, 128)
    )
    z_copies = []
    for d in range(15):
        cp = pltpu.make_async_remote_copy(
            src_ref=zb.at[(z + d + 1) % 16], dst_ref=rz.at[d],
            send_sem=zsend.at[d], recv_sem=zrecv.at[d],
            device_id=z_dev[d], device_id_type=MESH,
        )
        z_copies.append(cp)
    for d in (7, 6, 8, 5, 9, 4, 10, 3, 11, 2, 12, 1, 13, 0, 14):
        z_copies[d].start()

    for cp in g_copies:
        cp.wait()
    build_shifts(ghalo, even, odd, w, n)
    pre[...] = jnp.zeros((512, C), F32)
    for t in range(27):
        a, b, c = t // 9, (t // 3) % 3, t % 3
        pre[...] += jnp.dot(
            tap_rows(even, odd, 2 - a, 2 - b, 2 - c),
            wv[:, C * t : C * t + C],
            preferred_element_type=F32,
        )
    for xx in range(8):
        rows = slice(64 * xx, 64 * xx + 64)
        gin_ref[xx] = (pre[rows, :] * live[rows, :]).reshape(8, 8, C).astype(BF)

    total = zb[z].astype(F32)
    for d in range(15):
        z_copies[d].wait()
        total = total + rz[d].astype(F32)
    fin[...] = total * (1.0 / 512.0)

    g_all = []
    for d in (2, 4, 3, 0, 6, 1, 5):
        cp = pltpu.make_async_remote_copy(
            src_ref=fin, dst_ref=ag.at[n],
            send_sem=gsnd.at[d], recv_sem=grcv.at[d],
            device_id=n_dev[d], device_id_type=MESH,
        )
        cp.start()
        g_all.append(cp)
    ag[n] = fin[...]
    for cp in g_all:
        cp.wait()


def finish(act_in, gin_in, ag_in, act_out, gin_out, gw_out, ag, gw, sem):
    copies = [
        pltpu.make_async_copy(ag_in, ag, sem.at[0]),
        pltpu.make_async_copy(act_in, act_out, sem.at[1]),
        pltpu.make_async_copy(gin_in, gin_out, sem.at[2]),
    ]
    for cp in copies:
        cp.start()
    copies[0].wait()
    for m_ in range(8):
        for k in range(3):
            for t in range(5):
                lo = (5 * m_ + t) * 128
                gw[k : k + 1, lo : lo + 128] = ag[m_, 5 * k + t : 5 * k + t + 1, :]
    for k in range(3):
        gw[k : k + 1, 5120:5184] = ag[k, 15:16, 0:64]
    cp = pltpu.make_async_copy(gw, gw_out, sem.at[3])
    cp.start()
    copies[1].wait()
    copies[2].wait()
    cp.wait()


def local(features, weight, voxel_mask, cotangent):
    dma = pltpu.SemaphoreType.DMA
    vmem = pltpu.VMEM
    scratch = [
        vmem((C, 27 * C), BF),
        vmem((8, 8, 8), jnp.int32),
        vmem((8, 8, 8, C), BF),
        vmem((10, 10, 8, C), BF),
        vmem((10, 10, 8, C), BF),
        vmem((3, 10, 80, C), BF),
        vmem((3, 10, 64, C), BF),
        vmem((512, 5248), BF),
        vmem((512, C), F32),
        vmem((512, C), F32),
        vmem((512, C), BF),
        vmem((C, 512), BF),
        vmem((2, 4, 2, 16, 16, 128), F32),
        vmem((2, 4, 2, 16, 16, 128), BF),
        vmem((2, 4, 2, 16, 16, 128), BF),
        vmem((2, 4, 2, 16, 16, 128), BF),
        vmem((4, 8, 16, 128), F32),
        vmem((4, 8, 16, 128), F32),
        vmem((4, 8, 16, 128), BF),
        vmem((4, 8, 16, 128), BF),
        vmem((256, 128), BF),
        vmem((16, 16, 128), BF),
        vmem((16, 128), F32),
        vmem((4, 8, 16, 128), BF), vmem((4, 8, 16, 128), BF),
        vmem((2, 2, 8, 16, 128), BF), vmem((2, 2, 8, 16, 128), BF),
        vmem((4, 4, 16, 128), BF), vmem((4, 4, 16, 128), BF),
        vmem((2, 2, 4, 16, 128), BF), vmem((2, 2, 4, 16, 128), BF),
        vmem((3, 8, 16, 128), BF),
        vmem((3, 8, 16, 128), BF),
        vmem((15, 16, 128), BF),
        vmem((C, C), BF), vmem((256, 256), BF),
        dma((4,)),
        dma((8,)), dma((8,)), dma((8,)), dma((8,)),
        dma((8,)), dma((8,)),
        dma((2, 4)), dma((2, 4)), dma((2, 4)), dma((2, 4)), dma((2, 4)), dma((2, 4)),
        dma((2, 2)), dma((2, 2)), dma((2, 2)), dma((2, 2)), dma((2, 2)), dma((2, 2)),
        dma((3,)), dma((3,)), dma((3,)), dma((3,)),
        dma((15,)), dma((15,)),
        dma((7,)), dma((7,)),
        pltpu.SemaphoreType.REGULAR((3,)),
    ]
    any_ = pl.BlockSpec(memory_space=pl.ANY)
    hbm = pl.BlockSpec(memory_space=pltpu.HBM)
    vm = pl.BlockSpec(memory_space=pltpu.VMEM)
    act, gin, blocks = pl.pallas_call(
        kernel,
        name="sparse_conv",
        out_shape=(
            pltpu.VMEM((8, 8, 8, C), BF),
            pltpu.VMEM((8, 8, 8, C), BF),
            pltpu.VMEM((8, 16, 128), F32),
        ),
        in_specs=[hbm] * 4,
        out_specs=(vm, vm, vm),
        scratch_shapes=scratch,
        compiler_params=pltpu.CompilerParams(
            collective_id=0, has_side_effects=True, vmem_limit_bytes=61 * 1024 * 1024
        ),
    )(features, weight.T, voxel_mask, cotangent)
    return pl.pallas_call(
        finish,
        name="finish",
        out_shape=(
            jax.ShapeDtypeStruct((8, 8, 8, C), BF),
            jax.ShapeDtypeStruct((8, 8, 8, C), BF),
            jax.ShapeDtypeStruct((3, 27 * C), F32),
        ),
        in_specs=[any_] * 3,
        out_specs=(any_, any_, any_),
        scratch_shapes=[vmem((8, 16, 128), F32), vmem((3, 27 * C), F32), dma((4,))],
        compiler_params=pltpu.CompilerParams(vmem_limit_bytes=4 * 1024 * 1024),
    )(act, gin, blocks)


def solution(mesh):
    return jax.shard_map(
        local,
        mesh=mesh,
        in_specs=(
            P("wide", "narrow", None, None),
            P(),
            P("wide", "narrow", None),
            P("wide", "narrow", None, None),
        ),
        out_specs=(
            P("wide", "narrow", None, None),
            P("wide", "narrow", None, None),
            P("wide", None),
        ),
        check_vma=False,
    )
```

```python
import jax
import jax.numpy as jnp
from jax import lax
from jax.experimental import pallas as pl
from jax.experimental.pallas import tpu as pltpu
from jax.sharding import PartitionSpec as P

C = 192
BF = jnp.bfloat16
F32 = jnp.float32
MESH = pl.DeviceIdType.MESH
WIDE, NARROW = 64, 8
LAG = 3


def iota(shape, dim):
    return lax.broadcasted_iota(jnp.int32, shape, dim)


def build_shifts(src, even, odd, w, n):
    def body(x, carry):
        v = src[x].astype(F32)
        yy = iota((10, 8, C), 0)
        zz = iota((10, 8, C), 1)
        x_ok = jnp.logical_and(
            jnp.logical_or(x > 0, w > 0), jnp.logical_or(x < 9, w < WIDE - 1)
        )
        lo = jnp.where(n > 0, 0, 1)
        hi = jnp.where(n < NARROW - 1, 9, 8)
        lo = jnp.where(x_ok, lo, 100)
        v = jnp.where((yy >= lo) & (yy <= hi), v, 0.0)
        for c in range(3):
            if c == 0:
                s = jnp.where(zz == 0, 0.0, pltpu.roll(v, 1, 1))
            elif c == 1:
                s = v
            else:
                s = jnp.where(zz == 7, 0.0, pltpu.roll(v, 7, 1))
            s = s.reshape(80, C)
            even[c, x] = s.astype(BF)
            odd[c, x] = s[8:72].astype(BF)
        return carry

    lax.fori_loop(0, 10, body, 0)


def tap_rows(even, odd, a, b, c):
    if b == 1:
        v = odd[c, a : a + 8]
    else:
        v = even[c, a : a + 8, 8 * b : 8 * b + 64, :]
    return v.reshape(512, C)


def kernel(
    feat_hbm, w_hbm, mask_hbm, cot_hbm,
    act_ref, gin_ref, ag,
    wv, mask, cot, halo, ghalo, even, odd, cols, pre, live, gp2, gpt,
    own, sb, rb, s1b, a1, b1, a1b, b1b, tb, zb, fin,
    ra, rby, ra2, rb2, rz, permv, turnv,
    lsem, hsend, hrecv, gsend, grecv, csend, crecv,
    asend, arecv, bsend, brecv, a2send, a2recv, b2send, b2recv,
    zsend, zrecv, gsnd, grcv, ring,
):
    w = lax.axis_index("wide")
    n = lax.axis_index("narrow")
    core = w % 2
    xl = (w // 2) % 2
    z = w // 4
    y = n // 2
    xh = n % 2
    x = xh * 2 + xl

    def dev(z_, x_, c_, y_):
        return {"wide": (z_ * 2 + x_ % 2) * 2 + c_, "narrow": y_ * 2 + x_ // 2}

    near = []
    for dw, dn in ((1, 1), (1, -1), (-1, 1), (-1, -1), (0, 1), (0, -1), (1, 0), (-1, 0)):
        near.append(
            (dw, dn, {"wide": (w + dw + WIDE) % WIDE, "narrow": (n + dn + NARROW) % NARROW})
        )
    x_dev = [dev(z, (x + d) % 4, core, y) for d in (1, 2, 3)]
    y_dev = [dev(z, x, core, (y + d) % 4) for d in (1, 2, 3)]
    z_dev = [dev((z + d) % 16, x, core, y) for d in range(1, 16)]
    n_dev = [{"wide": w, "narrow": (n + d) % 8} for d in range(1, 8)]

    barrier = pltpu.get_barrier_semaphore()
    partners = [t[2] for t in near] + n_dev + x_dev + [z_dev[0], z_dev[14]]
    for p in partners:
        pl.semaphore_signal(barrier, inc=1, device_id=p, device_id_type=MESH)

    c_feat = pltpu.make_async_copy(feat_hbm, halo.at[1:9, 1:9], lsem.at[0])
    c_w = pltpu.make_async_copy(w_hbm, wv, lsem.at[1])
    c_cot = pltpu.make_async_copy(cot_hbm, cot, lsem.at[2])
    c_mask = pltpu.make_async_copy(mask_hbm, mask, lsem.at[3])
    c_mask.start()
    c_feat.start()
    c_w.start()
    c_cot.start()

    c_mask.wait()
    m = mask[...].astype(F32).reshape(64, 8).astype(BF)
    pick = (iota((512, 64), 0) // 8 == iota((512, 64), 1)).astype(F32).astype(BF)
    mm = jnp.dot(pick, m, preferred_element_type=F32)
    mm = jnp.where(iota((512, 8), 0) % 8 == iota((512, 8), 1), mm, 0.0).astype(BF)
    live[...] = jnp.dot(mm, jnp.ones((8, C), BF), preferred_element_type=F32)

    c_feat.wait()
    for xx in range(8):
        v = halo[1 + xx, 1:9].astype(F32) * live[64 * xx : 64 * xx + 64, :].reshape(8, 8, C)
        halo[1 + xx, 1:9] = v.astype(BF)

    pl.semaphore_wait(barrier, len(partners))

    def tell(d, k):
        for p in (z_dev[d - 1], z_dev[15 - d]):
            pl.semaphore_signal(ring.at[k], inc=1, device_id=p, device_id_type=MESH)

    def met(k):
        pl.semaphore_wait(ring.at[k], 2)

    tell(1, 0)

    def exchange(buf, send, recv):
        copies = []
        for k, (dw, dn, d) in enumerate(near):
            sx = {1: slice(8, 9), -1: slice(1, 2), 0: slice(1, 9)}[dw]
            tx = {1: slice(0, 1), -1: slice(9, 10), 0: slice(1, 9)}[dw]
            sy = {1: slice(8, 9), -1: slice(1, 2), 0: slice(1, 9)}[dn]
            ty = {1: slice(0, 1), -1: slice(9, 10), 0: slice(1, 9)}[dn]
            cp = pltpu.make_async_remote_copy(
                src_ref=buf.at[sx, sy],
                dst_ref=buf.at[tx, ty],
                send_sem=send.at[k],
                recv_sem=recv.at[k],
                device_id=d,
                device_id_type=MESH,
            )
            cp.start()
            copies.append(cp)
        return copies

    halo_copies = exchange(halo, hsend, hrecv)
    cols[:, 5120:5248] = jnp.zeros((512, 128), BF)
    r = iota((C, C), 0)
    q = (r >= 96).astype(jnp.int32)
    r = r - 96 * q
    rl = (r >= 48).astype(jnp.int32)
    r = r - 48 * rl
    rk = (r >= 16).astype(jnp.int32) + (r >= 32).astype(jnp.int32)
    rz_ = r - 16 * rk
    rc = jnp.where(q == 1, core, 1 - core)
    rj = 3 * ((rz_ * 2 + rl) * 2 + rc) + rk
    permv[...] = (rj == iota((C, C), 1)).astype(F32).astype(BF)
    rr = iota((256, 256), 0)
    turnv[...] = (iota((256, 256), 1) == (rr % 16) * 16 + rr // 16).astype(F32).astype(BF)

    for cp in halo_copies:
        cp.wait()
    met(0)
    tell(2, 1)

    build_shifts(halo, even, odd, w, n)
    for t in range(27):
        a, b, c = t // 9, (t // 3) % 3, t % 3
        cols[:, C * t : C * t + C] = tap_rows(even, odd, a, b, c)

    c_w.wait()
    pre[...] = lax.dot_general(
        cols[:, 0:5184], wv[...], (((1,), (1,)), ((), ())), preferred_element_type=F32
    )

    met(1)
    tell(4, 2)
    c_cot.wait()
    for xx in range(8):
        rows = slice(64 * xx, 64 * xx + 64)
        pv = pre[rows, :]
        lv = live[rows, :]
        sig = jax.nn.sigmoid(pv)
        act_ref[xx] = (pv * sig * lv).reshape(8, 8, C).astype(BF)
        slope = sig * (1.0 + pv * (1.0 - sig))
        ct = cot[xx].astype(F32).reshape(64, C)
        g = ct * lv * slope
        gp2[rows, :] = g.astype(BF)
        ghalo[1 + xx, 1:9] = g.reshape(8, 8, C).astype(BF)

    g_copies = exchange(ghalo, gsend, grecv)

    gpt[...] = lax.dot_general(
        permv[...], gp2[...], (((1,), (1,)), ((), ())), preferred_element_type=F32
    ).astype(BF)

    tail = jnp.dot(gpt[...], cols[:, 5120:5248], preferred_element_type=F32)
    for l_ in range(2):
        for m_ in range(8):
            k = m_ % 3
            lo = 48 * l_ + 16 * k
            sb[l_, m_ // 2, m_ % 2, 15] = tail[lo : lo + 16].astype(BF)
            own[l_, m_ // 2, m_ % 2, 15] = tail[96 + lo : 112 + lo]

    def owner(i):
        return (y + 2 + 3 * (i // 2)) % 4, (xh + 1 + i) % 2

    partner = dev(z, x, 1 - core, y)

    def core_copy(i):
        yy, hh = owner(i)
        return pltpu.make_async_remote_copy(
            src_ref=sb.at[:, yy, hh],
            dst_ref=rb.at[:, yy, hh],
            send_sem=csend.at[i],
            recv_sem=crecv.at[i],
            device_id=partner,
            device_id_type=MESH,
        )

    def wgrad(i, carry):
        yy, hh = owner(i)
        col = pl.multiple_of((yy * 2 + hh) * 640, 128)
        o = jnp.dot(gpt[...], cols[:, pl.ds(col, 640)], preferred_element_type=F32)
        for l_ in range(2):
            for k in range(3):
                lo = 48 * l_ + 16 * k
                for t in range(5):
                    sb[l_, yy, hh, 5 * k + t] = o[lo : lo + 16, 128 * t : 128 * t + 128].astype(BF)
                    own[l_, yy, hh, 5 * k + t] = o[96 + lo : 112 + lo, 128 * t : 128 * t + 128]
        core_copy(i).start()
        return carry

    def a_copy(i, l_):
        yy, hh = owner(i)
        xt = hh * 2 + l_
        d = (xt - x + 4) % 4
        return d != 0, pltpu.make_async_remote_copy(
            src_ref=s1b.at[l_, yy, hh, pl.ds(0, 8)],
            dst_ref=ra.at[jnp.maximum(d - 1, 0), yy],
            send_sem=asend.at[i, l_],
            recv_sem=arecv.at[jnp.maximum(d - 1, 0), yy],
            device_id=dev(z, xt, core, y),
            device_id_type=MESH,
        )

    def b_copy(i):
        yy, hh = owner(i)
        d = (yy - y + 4) % 4
        return d != 0, pltpu.make_async_remote_copy(
            src_ref=s1b.at[:, yy, hh, pl.ds(8, 8)],
            dst_ref=rby.at[jnp.maximum(d - 1, 0), :, hh],
            send_sem=bsend.at[i],
            recv_sem=brecv.at[jnp.maximum(d - 1, 0), hh],
            device_id=dev(z, x, core, yy),
            device_id_type=MESH,
        )

    def first(i, carry):
        yy, hh = owner(i)
        core_copy(i).wait()
        for l_ in range(2):
            s = own[l_, yy, hh] + rb[l_, yy, hh].astype(F32)
            own[l_, yy, hh] = s
            s1b[l_, yy, hh] = s.astype(BF)
        for l_ in range(2):
            go, cp = a_copy(i, l_)
            pl.when(go)(cp.start)
        go, cp = b_copy(i)
        pl.when(go)(cp.start)
        return carry

    def both(i, carry):
        wgrad(i, carry)
        first(i - LAG, carry)
        return carry

    lax.fori_loop(0, LAG, wgrad, 0)
    lax.fori_loop(LAG, 8, both, 0)
    lax.fori_loop(8 - LAG, 8, first, 0)
    def first_wait(i, carry):
        for l_ in range(2):
            go, cp = a_copy(i, l_)
            pl.when(go)(cp.wait_send)
        go, cp = b_copy(i)
        pl.when(go)(cp.wait_send)
        return carry

    for d in range(3):
        for yy in range(4):
            pltpu.make_async_remote_copy(
                src_ref=s1b.at[0, yy, 0, pl.ds(0, 8)], dst_ref=ra.at[d, yy],
                send_sem=asend.at[0, 0], recv_sem=arecv.at[d, yy],
                device_id=partner, device_id_type=MESH,
            ).wait_recv()
        for hh in range(2):
            pltpu.make_async_remote_copy(
                src_ref=s1b.at[:, 0, hh, pl.ds(8, 8)], dst_ref=rby.at[d, :, hh],
                send_sem=bsend.at[0], recv_sem=brecv.at[d, hh],
                device_id=partner, device_id_type=MESH,
            ).wait_recv()

    for yy in range(4):
        s = own[xl, yy, xh, 0:8]
        for d in range(3):
            s = s + ra[d, yy].astype(F32)
        a1[yy] = s
        a1b[yy] = s.astype(BF)
    for l_ in range(2):
        for hh in range(2):
            s = own[l_, y, hh, 8:16]
            for d in range(3):
                s = s + rby[d, l_, hh].astype(F32)
            b1[hh * 2 + l_] = s
            b1b[hh * 2 + l_] = s.astype(BF)

    second = []
    for d in (1, 0, 2):
        second.append(
            pltpu.make_async_remote_copy(
                src_ref=a1b.at[(y + d + 1) % 4], dst_ref=ra2.at[d],
                send_sem=a2send.at[d], recv_sem=a2recv.at[d],
                device_id=y_dev[d], device_id_type=MESH,
            )
        )
        second.append(
            pltpu.make_async_remote_copy(
                src_ref=b1b.at[(x + d + 1) % 4], dst_ref=rb2.at[d],
                send_sem=b2send.at[d], recv_sem=b2recv.at[d],
                device_id=x_dev[d], device_id_type=MESH,
            )
        )
    for cp in second:
        cp.start()
    met(2)
    lax.fori_loop(0, 8, first_wait, 0)
    for cp in second:
        cp.wait()
    sa = a1[y]
    sbb = b1[x]
    for d in range(3):
        sa = sa + ra2[d].astype(F32)
        sbb = sbb + rb2[d].astype(F32)
    tb[0:128] = sa.reshape(128, 128).astype(BF)
    tb[128:256] = sbb.reshape(128, 128).astype(BF)

    zb[...] = (
        jnp.dot(turnv[...], tb[...], preferred_element_type=F32).astype(BF).reshape(16, 16, 128)
    )
    z_copies = []
    for d in range(15):
        cp = pltpu.make_async_remote_copy(
            src_ref=zb.at[(z + d + 1) % 16], dst_ref=rz.at[d],
            send_sem=zsend.at[d], recv_sem=zrecv.at[d],
            device_id=z_dev[d], device_id_type=MESH,
        )
        z_copies.append(cp)
    for d in (7, 6, 8, 5, 9, 4, 10, 3, 11, 2, 12, 1, 13, 0, 14):
        z_copies[d].start()

    for cp in g_copies:
        cp.wait()
    build_shifts(ghalo, even, odd, w, n)
    pre[...] = jnp.zeros((512, C), F32)
    for t in range(27):
        a, b, c = t // 9, (t // 3) % 3, t % 3
        pre[...] += jnp.dot(
            tap_rows(even, odd, 2 - a, 2 - b, 2 - c),
            wv[:, C * t : C * t + C],
            preferred_element_type=F32,
        )
    for xx in range(8):
        rows = slice(64 * xx, 64 * xx + 64)
        gin_ref[xx] = (pre[rows, :] * live[rows, :]).reshape(8, 8, C).astype(BF)

    total = zb[z].astype(F32)
    for d in range(15):
        z_copies[d].wait()
        total = total + rz[d].astype(F32)
    fin[...] = total * (1.0 / 512.0)

    g_all = []
    for d in (2, 4, 3, 0, 6, 1, 5):
        cp = pltpu.make_async_remote_copy(
            src_ref=fin, dst_ref=ag.at[n],
            send_sem=gsnd.at[d], recv_sem=grcv.at[d],
            device_id=n_dev[d], device_id_type=MESH,
        )
        cp.start()
        g_all.append(cp)
    ag[n] = fin[...]
    for cp in g_all:
        cp.wait()


def finish(act_in, gin_in, ag_in, act_out, gin_out, gw_out, ag, gw, sem):
    copies = [
        pltpu.make_async_copy(ag_in, ag, sem.at[0]),
        pltpu.make_async_copy(act_in, act_out, sem.at[1]),
        pltpu.make_async_copy(gin_in, gin_out, sem.at[2]),
    ]
    for cp in copies:
        cp.start()
    copies[0].wait()
    for m_ in range(8):
        for k in range(3):
            for t in range(5):
                lo = (5 * m_ + t) * 128
                gw[k : k + 1, lo : lo + 128] = ag[m_, 5 * k + t : 5 * k + t + 1, :]
    for k in range(3):
        gw[k : k + 1, 5120:5184] = ag[k, 15:16, 0:64]
    cp = pltpu.make_async_copy(gw, gw_out, sem.at[3])
    cp.start()
    copies[1].wait()
    copies[2].wait()
    cp.wait()


def local(features, weight, voxel_mask, cotangent):
    dma = pltpu.SemaphoreType.DMA
    vmem = pltpu.VMEM
    scratch = [
        vmem((C, 27 * C), BF),
        vmem((8, 8, 8), jnp.int32),
        vmem((8, 8, 8, C), BF),
        vmem((10, 10, 8, C), BF),
        vmem((10, 10, 8, C), BF),
        vmem((3, 10, 80, C), BF),
        vmem((3, 10, 64, C), BF),
        vmem((512, 5248), BF),
        vmem((512, C), F32),
        vmem((512, C), F32),
        vmem((512, C), BF),
        vmem((C, 512), BF),
        vmem((2, 4, 2, 16, 16, 128), F32),
        vmem((2, 4, 2, 16, 16, 128), BF),
        vmem((2, 4, 2, 16, 16, 128), BF),
        vmem((2, 4, 2, 16, 16, 128), BF),
        vmem((4, 8, 16, 128), F32),
        vmem((4, 8, 16, 128), F32),
        vmem((4, 8, 16, 128), BF),
        vmem((4, 8, 16, 128), BF),
        vmem((256, 128), BF),
        vmem((16, 16, 128), BF),
        vmem((16, 128), F32),
        vmem((3, 4, 8, 16, 128), BF),
        vmem((3, 2, 2, 8, 16, 128), BF),
        vmem((3, 8, 16, 128), BF),
        vmem((3, 8, 16, 128), BF),
        vmem((15, 16, 128), BF),
        vmem((C, C), BF), vmem((256, 256), BF),
        dma((4,)),
        dma((8,)), dma((8,)), dma((8,)), dma((8,)),
        dma((8,)), dma((8,)),
        dma((8, 2)), dma((3, 4)),
        dma((8,)), dma((3, 2)),
        dma((3,)), dma((3,)), dma((3,)), dma((3,)),
        dma((15,)), dma((15,)),
        dma((7,)), dma((7,)),
        pltpu.SemaphoreType.REGULAR((3,)),
    ]
    any_ = pl.BlockSpec(memory_space=pl.ANY)
    hbm = pl.BlockSpec(memory_space=pltpu.HBM)
    vm = pl.BlockSpec(memory_space=pltpu.VMEM)
    act, gin, blocks = pl.pallas_call(
        kernel,
        name="sparse_conv",
        out_shape=(
            pltpu.VMEM((8, 8, 8, C), BF),
            pltpu.VMEM((8, 8, 8, C), BF),
            pltpu.VMEM((8, 16, 128), F32),
        ),
        in_specs=[hbm] * 4,
        out_specs=(vm, vm, vm),
        scratch_shapes=scratch,
        compiler_params=pltpu.CompilerParams(
            collective_id=0, has_side_effects=True, vmem_limit_bytes=61 * 1024 * 1024
        ),
    )(features, weight.T, voxel_mask, cotangent)
    return pl.pallas_call(
        finish,
        name="finish",
        out_shape=(
            jax.ShapeDtypeStruct((8, 8, 8, C), BF),
            jax.ShapeDtypeStruct((8, 8, 8, C), BF),
            jax.ShapeDtypeStruct((3, 27 * C), F32),
        ),
        in_specs=[any_] * 3,
        out_specs=(any_, any_, any_),
        scratch_shapes=[vmem((8, 16, 128), F32), vmem((3, 27 * C), F32), dma((4,))],
        compiler_params=pltpu.CompilerParams(vmem_limit_bytes=4 * 1024 * 1024),
    )(act, gin, blocks)


def solution(mesh):
    return jax.shard_map(
        local,
        mesh=mesh,
        in_specs=(
            P("wide", "narrow", None, None),
            P(),
            P("wide", "narrow", None),
            P("wide", "narrow", None, None),
        ),
        out_specs=(
            P("wide", "narrow", None, None),
            P("wide", "narrow", None, None),
            P("wide", None),
        ),
        check_vma=False,
    )
```

```python
import jax
import jax.numpy as jnp
from jax import lax
from jax.experimental import pallas as pl
from jax.experimental.pallas import tpu as pltpu
from jax.sharding import PartitionSpec as P

C = 192
BF = jnp.bfloat16
F32 = jnp.float32
MESH = pl.DeviceIdType.MESH
WIDE, NARROW = 64, 8
LAG = 2


def iota(shape, dim):
    return lax.broadcasted_iota(jnp.int32, shape, dim)


def build_shifts(src, even, odd, w, n):
    def body(x, carry):
        v = src[x].astype(F32)
        yy = iota((10, 8, C), 0)
        zz = iota((10, 8, C), 1)
        x_ok = jnp.logical_and(
            jnp.logical_or(x > 0, w > 0), jnp.logical_or(x < 9, w < WIDE - 1)
        )
        lo = jnp.where(n > 0, 0, 1)
        hi = jnp.where(n < NARROW - 1, 9, 8)
        lo = jnp.where(x_ok, lo, 100)
        v = jnp.where((yy >= lo) & (yy <= hi), v, 0.0)
        for c in range(3):
            if c == 0:
                s = jnp.where(zz == 0, 0.0, pltpu.roll(v, 1, 1))
            elif c == 1:
                s = v
            else:
                s = jnp.where(zz == 7, 0.0, pltpu.roll(v, 7, 1))
            s = s.reshape(80, C)
            even[c, x] = s.astype(BF)
            odd[c, x] = s[8:72].astype(BF)
        return carry

    lax.fori_loop(0, 10, body, 0)


def tap_rows(even, odd, a, b, c):
    if b == 1:
        v = odd[c, a : a + 8]
    else:
        v = even[c, a : a + 8, 8 * b : 8 * b + 64, :]
    return v.reshape(512, C)


def kernel(
    feat_hbm, w_hbm, mask_hbm, cot_hbm,
    act_ref, gin_ref, ag,
    wv, mask, cot, halo, ghalo, even, odd, cols, pre, live, gp2, gpt,
    own, sb, rb, s1b, a1, b1, a1b, b1b, tb, zb, fin,
    ra, rby, ra2, rb2, rz, permv, turnv,
    lsem, hsend, hrecv, gsend, grecv, csend, crecv,
    asend, arecv, bsend, brecv, a2send, a2recv, b2send, b2recv,
    zsend, zrecv, gsnd, grcv, ring,
):
    w = lax.axis_index("wide")
    n = lax.axis_index("narrow")
    core = w % 2
    xl = (w // 2) % 2
    z = w // 4
    y = n // 2
    xh = n % 2
    x = xh * 2 + xl

    def dev(z_, x_, c_, y_):
        return {"wide": (z_ * 2 + x_ % 2) * 2 + c_, "narrow": y_ * 2 + x_ // 2}

    near = []
    for dw, dn in ((1, 1), (1, -1), (-1, 1), (-1, -1), (0, 1), (0, -1), (1, 0), (-1, 0)):
        near.append(
            (dw, dn, {"wide": (w + dw + WIDE) % WIDE, "narrow": (n + dn + NARROW) % NARROW})
        )
    x_dev = [dev(z, (x + d) % 4, core, y) for d in (1, 2, 3)]
    y_dev = [dev(z, x, core, (y + d) % 4) for d in (1, 2, 3)]
    z_dev = [dev((z + d) % 16, x, core, y) for d in range(1, 16)]
    n_dev = [{"wide": w, "narrow": (n + d) % 8} for d in range(1, 8)]

    barrier = pltpu.get_barrier_semaphore()
    partners = [t[2] for t in near] + n_dev[1:6] + x_dev + [z_dev[0], z_dev[14]]
    for p in partners:
        pl.semaphore_signal(barrier, inc=1, device_id=p, device_id_type=MESH)

    c_feat = pltpu.make_async_copy(feat_hbm, halo.at[1:9, 1:9], lsem.at[0])
    c_w = pltpu.make_async_copy(w_hbm, wv, lsem.at[1])
    c_cot = pltpu.make_async_copy(cot_hbm, cot, lsem.at[2])
    c_mask = pltpu.make_async_copy(mask_hbm, mask, lsem.at[3])
    c_mask.start()
    c_feat.start()
    c_w.start()
    c_cot.start()

    c_mask.wait()
    m = mask[...].astype(F32).reshape(64, 8).astype(BF)
    pick = (iota((512, 64), 0) // 8 == iota((512, 64), 1)).astype(F32).astype(BF)
    mm = jnp.dot(pick, m, preferred_element_type=F32)
    mm = jnp.where(iota((512, 8), 0) % 8 == iota((512, 8), 1), mm, 0.0).astype(BF)
    live[...] = jnp.dot(mm, jnp.ones((8, C), BF), preferred_element_type=F32)

    c_feat.wait()
    for xx in range(8):
        v = halo[1 + xx, 1:9].astype(F32) * live[64 * xx : 64 * xx + 64, :].reshape(8, 8, C)
        halo[1 + xx, 1:9] = v.astype(BF)

    pl.semaphore_wait(barrier, len(partners))

    def tell(d, k):
        for p in (z_dev[d - 1], z_dev[15 - d]):
            pl.semaphore_signal(ring.at[k], inc=1, device_id=p, device_id_type=MESH)

    def met(k):
        pl.semaphore_wait(ring.at[k], 2)

    tell(1, 0)

    def exchange(buf, send, recv):
        copies = []
        for k, (dw, dn, d) in enumerate(near):
            sx = {1: slice(8, 9), -1: slice(1, 2), 0: slice(1, 9)}[dw]
            tx = {1: slice(0, 1), -1: slice(9, 10), 0: slice(1, 9)}[dw]
            sy = {1: slice(8, 9), -1: slice(1, 2), 0: slice(1, 9)}[dn]
            ty = {1: slice(0, 1), -1: slice(9, 10), 0: slice(1, 9)}[dn]
            cp = pltpu.make_async_remote_copy(
                src_ref=buf.at[sx, sy],
                dst_ref=buf.at[tx, ty],
                send_sem=send.at[k],
                recv_sem=recv.at[k],
                device_id=d,
                device_id_type=MESH,
            )
            cp.start()
            copies.append(cp)
        return copies

    halo_copies = exchange(halo, hsend, hrecv)
    cols[:, 5120:5248] = jnp.zeros((512, 128), BF)
    r = iota((C, C), 0)
    q = (r >= 96).astype(jnp.int32)
    r = r - 96 * q
    rl = (r >= 48).astype(jnp.int32)
    r = r - 48 * rl
    rk = (r >= 16).astype(jnp.int32) + (r >= 32).astype(jnp.int32)
    rz_ = r - 16 * rk
    rc = jnp.where(q == 1, core, 1 - core)
    rj = 3 * ((rz_ * 2 + rl) * 2 + rc) + rk
    permv[...] = (rj == iota((C, C), 1)).astype(F32).astype(BF)
    rr = iota((256, 256), 0)
    turnv[...] = (iota((256, 256), 1) == (rr % 16) * 16 + rr // 16).astype(F32).astype(BF)

    for cp in halo_copies:
        cp.wait()
    met(0)
    tell(2, 1)

    build_shifts(halo, even, odd, w, n)
    for t in range(27):
        a, b, c = t // 9, (t // 3) % 3, t % 3
        cols[:, C * t : C * t + C] = tap_rows(even, odd, a, b, c)

    c_w.wait()
    pre[...] = lax.dot_general(
        cols[:, 0:5184], wv[...], (((1,), (1,)), ((), ())), preferred_element_type=F32
    )

    met(1)
    tell(4, 2)
    c_cot.wait()
    for xx in range(8):
        rows = slice(64 * xx, 64 * xx + 64)
        pv = pre[rows, :]
        lv = live[rows, :]
        sig = jax.nn.sigmoid(pv)
        act_ref[xx] = (pv * sig * lv).reshape(8, 8, C).astype(BF)
        slope = sig * (1.0 + pv * (1.0 - sig))
        ct = cot[xx].astype(F32).reshape(64, C)
        g = ct * lv * slope
        gp2[rows, :] = g.astype(BF)
        ghalo[1 + xx, 1:9] = g.reshape(8, 8, C).astype(BF)

    g_copies = exchange(ghalo, gsend, grecv)

    gpt[...] = lax.dot_general(
        permv[...], gp2[...], (((1,), (1,)), ((), ())), preferred_element_type=F32
    ).astype(BF)

    tail = jnp.dot(gpt[...], cols[:, 5120:5248], preferred_element_type=F32)
    for l_ in range(2):
        for m_ in range(8):
            k = m_ % 3
            lo = 48 * l_ + 16 * k
            sb[l_, m_ // 2, m_ % 2, 15] = tail[lo : lo + 16].astype(BF)
            own[l_, m_ // 2, m_ % 2, 15] = tail[96 + lo : 112 + lo]

    def owner(i):
        return (y + 2 + 3 * (i // 2)) % 4, (xh + 1 + i) % 2

    partner = dev(z, x, 1 - core, y)

    def core_copy(i):
        yy, hh = owner(i)
        return pltpu.make_async_remote_copy(
            src_ref=sb.at[:, yy, hh],
            dst_ref=rb.at[:, yy, hh],
            send_sem=csend.at[i],
            recv_sem=crecv.at[i],
            device_id=partner,
            device_id_type=MESH,
        )

    def wgrad(i, carry):
        yy, hh = owner(i)
        col = pl.multiple_of((yy * 2 + hh) * 640, 128)
        o = jnp.dot(gpt[...], cols[:, pl.ds(col, 640)], preferred_element_type=F32)
        for l_ in range(2):
            for k in range(3):
                lo = 48 * l_ + 16 * k
                for t in range(5):
                    sb[l_, yy, hh, 5 * k + t] = o[lo : lo + 16, 128 * t : 128 * t + 128].astype(BF)
                    own[l_, yy, hh, 5 * k + t] = o[96 + lo : 112 + lo, 128 * t : 128 * t + 128]
        core_copy(i).start()
        return carry

    def a_copy(i, l_):
        yy, hh = owner(i)
        xt = hh * 2 + l_
        d = (xt - x + 4) % 4
        return d != 0, pltpu.make_async_remote_copy(
            src_ref=s1b.at[l_, yy, hh, pl.ds(0, 8)],
            dst_ref=ra.at[jnp.maximum(d - 1, 0), yy],
            send_sem=asend.at[i, l_],
            recv_sem=arecv.at[jnp.maximum(d - 1, 0), yy],
            device_id=dev(z, xt, core, y),
            device_id_type=MESH,
        )

    def b_copy(i):
        yy, hh = owner(i)
        d = (yy - y + 4) % 4
        return d != 0, pltpu.make_async_remote_copy(
            src_ref=s1b.at[:, yy, hh, pl.ds(8, 8)],
            dst_ref=rby.at[jnp.maximum(d - 1, 0), :, hh],
            send_sem=bsend.at[i],
            recv_sem=brecv.at[jnp.maximum(d - 1, 0), hh],
            device_id=dev(z, x, core, yy),
            device_id_type=MESH,
        )

    def first(i, carry):
        yy, hh = owner(i)
        core_copy(i).wait()
        for l_ in range(2):
            s = own[l_, yy, hh] + rb[l_, yy, hh].astype(F32)
            own[l_, yy, hh] = s
            s1b[l_, yy, hh] = s.astype(BF)
        for l_ in range(2):
            go, cp = a_copy(i, l_)
            pl.when(go)(cp.start)
        go, cp = b_copy(i)
        pl.when(go)(cp.start)
        return carry

    def both(i, carry):
        wgrad(i, carry)
        first(i - LAG, carry)
        return carry

    lax.fori_loop(0, LAG, wgrad, 0)
    lax.fori_loop(LAG, 8, both, 0)
    lax.fori_loop(8 - LAG, 8, first, 0)
    def first_wait(i, carry):
        for l_ in range(2):
            go, cp = a_copy(i, l_)
            pl.when(go)(cp.wait_send)
        go, cp = b_copy(i)
        pl.when(go)(cp.wait_send)
        return carry

    for d in range(3):
        for yy in range(4):
            pltpu.make_async_remote_copy(
                src_ref=s1b.at[0, yy, 0, pl.ds(0, 8)], dst_ref=ra.at[d, yy],
                send_sem=asend.at[0, 0], recv_sem=arecv.at[d, yy],
                device_id=partner, device_id_type=MESH,
            ).wait_recv()
        for hh in range(2):
            pltpu.make_async_remote_copy(
                src_ref=s1b.at[:, 0, hh, pl.ds(8, 8)], dst_ref=rby.at[d, :, hh],
                send_sem=bsend.at[0], recv_sem=brecv.at[d, hh],
                device_id=partner, device_id_type=MESH,
            ).wait_recv()

    for yy in range(4):
        s = own[xl, yy, xh, 0:8]
        for d in range(3):
            s = s + ra[d, yy].astype(F32)
        a1[yy] = s
        a1b[yy] = s.astype(BF)
    for l_ in range(2):
        for hh in range(2):
            s = own[l_, y, hh, 8:16]
            for d in range(3):
                s = s + rby[d, l_, hh].astype(F32)
            b1[hh * 2 + l_] = s
            b1b[hh * 2 + l_] = s.astype(BF)

    second = []
    for d in (1, 0, 2):
        second.append(
            pltpu.make_async_remote_copy(
                src_ref=a1b.at[(y + d + 1) % 4], dst_ref=ra2.at[d],
                send_sem=a2send.at[d], recv_sem=a2recv.at[d],
                device_id=y_dev[d], device_id_type=MESH,
            )
        )
        second.append(
            pltpu.make_async_remote_copy(
                src_ref=b1b.at[(x + d + 1) % 4], dst_ref=rb2.at[d],
                send_sem=b2send.at[d], recv_sem=b2recv.at[d],
                device_id=x_dev[d], device_id_type=MESH,
            )
        )
    for cp in second:
        cp.start()
    met(2)
    lax.fori_loop(0, 8, first_wait, 0)
    for cp in second:
        cp.wait()
    sa = a1[y]
    sbb = b1[x]
    for d in range(3):
        sa = sa + ra2[d].astype(F32)
        sbb = sbb + rb2[d].astype(F32)
    tb[0:128] = sa.reshape(128, 128).astype(BF)
    tb[128:256] = sbb.reshape(128, 128).astype(BF)

    zb[...] = (
        jnp.dot(turnv[...], tb[...], preferred_element_type=F32).astype(BF).reshape(16, 16, 128)
    )
    z_copies = []
    for d in range(15):
        cp = pltpu.make_async_remote_copy(
            src_ref=zb.at[(z + d + 1) % 16], dst_ref=rz.at[d],
            send_sem=zsend.at[d], recv_sem=zrecv.at[d],
            device_id=z_dev[d], device_id_type=MESH,
        )
        z_copies.append(cp)
    for d in (7, 6, 8, 5, 9, 4, 10, 3, 11, 2, 12, 1, 13, 0, 14):
        z_copies[d].start()

    for cp in g_copies:
        cp.wait()
    build_shifts(ghalo, even, odd, w, n)
    pre[...] = jnp.zeros((512, C), F32)
    for t in range(27):
        a, b, c = t // 9, (t // 3) % 3, t % 3
        pre[...] += jnp.dot(
            tap_rows(even, odd, 2 - a, 2 - b, 2 - c),
            wv[:, C * t : C * t + C],
            preferred_element_type=F32,
        )
    for xx in range(8):
        rows = slice(64 * xx, 64 * xx + 64)
        gin_ref[xx] = (pre[rows, :] * live[rows, :]).reshape(8, 8, C).astype(BF)

    total = zb[z].astype(F32)
    for d in range(15):
        z_copies[d].wait()
        total = total + rz[d].astype(F32)
    fin[...] = total * (1.0 / 512.0)

    g_all = []
    for d in (2, 4, 3, 0, 6, 1, 5):
        cp = pltpu.make_async_remote_copy(
            src_ref=fin, dst_ref=ag.at[n],
            send_sem=gsnd.at[d], recv_sem=grcv.at[d],
            device_id=n_dev[d], device_id_type=MESH,
        )
        cp.start()
        g_all.append(cp)
    ag[n] = fin[...]
    for cp in g_all:
        cp.wait()


def finish(act_in, gin_in, ag_in, act_out, gin_out, gw_out, ag, gw, sem):
    copies = [
        pltpu.make_async_copy(ag_in, ag, sem.at[0]),
        pltpu.make_async_copy(act_in, act_out, sem.at[1]),
        pltpu.make_async_copy(gin_in, gin_out, sem.at[2]),
    ]
    for cp in copies:
        cp.start()
    copies[0].wait()
    for m_ in range(8):
        for k in range(3):
            for t in range(5):
                lo = (5 * m_ + t) * 128
                gw[k : k + 1, lo : lo + 128] = ag[m_, 5 * k + t : 5 * k + t + 1, :]
    for k in range(3):
        gw[k : k + 1, 5120:5184] = ag[k, 15:16, 0:64]
    cp = pltpu.make_async_copy(gw, gw_out, sem.at[3])
    cp.start()
    copies[1].wait()
    copies[2].wait()
    cp.wait()


def local(features, weight, voxel_mask, cotangent):
    dma = pltpu.SemaphoreType.DMA
    vmem = pltpu.VMEM
    scratch = [
        vmem((C, 27 * C), BF),
        vmem((8, 8, 8), jnp.int32),
        vmem((8, 8, 8, C), BF),
        vmem((10, 10, 8, C), BF),
        vmem((10, 10, 8, C), BF),
        vmem((3, 10, 80, C), BF),
        vmem((3, 10, 64, C), BF),
        vmem((512, 5248), BF),
        vmem((512, C), F32),
        vmem((512, C), F32),
        vmem((512, C), BF),
        vmem((C, 512), BF),
        vmem((2, 4, 2, 16, 16, 128), F32),
        vmem((2, 4, 2, 16, 16, 128), BF),
        vmem((2, 4, 2, 16, 16, 128), BF),
        vmem((2, 4, 2, 16, 16, 128), BF),
        vmem((4, 8, 16, 128), F32),
        vmem((4, 8, 16, 128), F32),
        vmem((4, 8, 16, 128), BF),
        vmem((4, 8, 16, 128), BF),
        vmem((256, 128), BF),
        vmem((16, 16, 128), BF),
        vmem((16, 128), F32),
        vmem((3, 4, 8, 16, 128), BF),
        vmem((3, 2, 2, 8, 16, 128), BF),
        vmem((3, 8, 16, 128), BF),
        vmem((3, 8, 16, 128), BF),
        vmem((15, 16, 128), BF),
        vmem((C, C), BF), vmem((256, 256), BF),
        dma((4,)),
        dma((8,)), dma((8,)), dma((8,)), dma((8,)),
        dma((8,)), dma((8,)),
        dma((8, 2)), dma((3, 4)),
        dma((8,)), dma((3, 2)),
        dma((3,)), dma((3,)), dma((3,)), dma((3,)),
        dma((15,)), dma((15,)),
        dma((7,)), dma((7,)),
        pltpu.SemaphoreType.REGULAR((3,)),
    ]
    any_ = pl.BlockSpec(memory_space=pl.ANY)
    hbm = pl.BlockSpec(memory_space=pltpu.HBM)
    vm = pl.BlockSpec(memory_space=pltpu.VMEM)
    act, gin, blocks = pl.pallas_call(
        kernel,
        name="sparse_conv",
        out_shape=(
            pltpu.VMEM((8, 8, 8, C), BF),
            pltpu.VMEM((8, 8, 8, C), BF),
            pltpu.VMEM((8, 16, 128), F32),
        ),
        in_specs=[hbm] * 4,
        out_specs=(vm, vm, vm),
        scratch_shapes=scratch,
        compiler_params=pltpu.CompilerParams(
            collective_id=0, has_side_effects=True, vmem_limit_bytes=61 * 1024 * 1024
        ),
    )(features, weight.T, voxel_mask, cotangent)
    return pl.pallas_call(
        finish,
        name="finish",
        out_shape=(
            jax.ShapeDtypeStruct((8, 8, 8, C), BF),
            jax.ShapeDtypeStruct((8, 8, 8, C), BF),
            jax.ShapeDtypeStruct((3, 27 * C), F32),
        ),
        in_specs=[any_] * 3,
        out_specs=(any_, any_, any_),
        scratch_shapes=[vmem((8, 16, 128), F32), vmem((3, 27 * C), F32), dma((4,))],
        compiler_params=pltpu.CompilerParams(vmem_limit_bytes=4 * 1024 * 1024),
    )(act, gin, blocks)


def solution(mesh):
    return jax.shard_map(
        local,
        mesh=mesh,
        in_specs=(
            P("wide", "narrow", None, None),
            P(),
            P("wide", "narrow", None),
            P("wide", "narrow", None, None),
        ),
        out_specs=(
            P("wide", "narrow", None, None),
            P("wide", "narrow", None, None),
            P("wide", None),
        ),
        check_vma=False,
    )
```
